32 devices in a mesh: tm: 8 (over z, x), col: 4 (over y, core).
Axes of the slice: x: 2, y: 2, z: 4, core: 2. Of those that a mesh axis runs over, the one named last changes fastest.
Arguments:
- near_prop: bfloat16 [16, 2, 512, 512], P('tm', None, None, 'col'), may hold values from -0.1875 to 0.1875
- far_prop: bfloat16 [16, 2, 512, 512], P('tm', None, None, 'col'), may hold values from -0.1875 to 0.1875
- meson: bfloat16 [16, 2, 512, 512], P('tm', None, None, 'col'), may hold values from -6 to 6
Outputs:
- blocks: float32 [16, 2, 512, 512], P('tm', None, None, 'col')
The draws below stay inside these ranges and needn't reach their ends.
All inputs are finite; a program needn't handle non-finite values.
Results may differ from the reference program's by a relative error of at most 0.0035.
Values may be sent and summed in bfloat16 or wider, within the bound.
A program may use at most 64 MiB of HBM per device.

```python
import jax
import jax.numpy as jnp
from jax import lax

NO = 512
TIMES = 16
SEP_NEAR = 2
SEP_FAR = 6


def block_levels(stream_key, shape, shards, least, high):
    level = 1.0
    for dim, blocks in shards:
        heights = jax.random.uniform(jax.random.fold_in(jax.random.fold_in(stream_key, 6), dim), (blocks,), jnp.float32, least / len(shards), high / len(shards))
        level = level * jnp.repeat(jnp.exp(heights), shape[dim] // blocks).reshape((-1,) + (1,) * (len(shape) - 1 - dim))
    return level


def gaussian(key, shape, scale, bound, shards=(), dtype=jnp.bfloat16):
    values = jax.random.normal(key, shape, jnp.float32) * scale
    if len(shards) > 0:
        values = block_levels(key, shape, shards, -0.22, 0.18) * values
    return jnp.clip(values, min=-bound, max=bound).astype(dtype)


def setup_inputs(seed: int = 0) -> dict:
    streams_of = jax.random.split(jax.random.key(seed), 4)
    near_prop = gaussian(streams_of[0], (TIMES, 2, NO, NO), (2 * NO) ** -0.5, 0.1875, ((0, 8), (3, 4)))
    far_prop = gaussian(streams_of[1], (TIMES, 2, NO, NO), (2 * NO) ** -0.5, 0.1875, ((0, 8), (3, 4)))
    meson = gaussian(streams_of[2], (TIMES, 2, NO, NO), 1.0, 6.0, ((0, 8), (3, 4)))
    return dict(near_prop=near_prop, far_prop=far_prop, meson=meson)


def complex_product(left, right):
    real_part = jnp.einsum("tik,tkj->tij", left[:, 0], right[:, 0], precision=lax.Precision.HIGHEST) - jnp.einsum("tik,tkj->tij", left[:, 1], right[:, 1], precision=lax.Precision.HIGHEST)
    imag_part = jnp.einsum("tik,tkj->tij", left[:, 0], right[:, 1], precision=lax.Precision.HIGHEST) + jnp.einsum("tik,tkj->tij", left[:, 1], right[:, 0], precision=lax.Precision.HIGHEST)
    return jnp.stack([real_part, imag_part], axis=1)


def to_half(value):
    rounded = value.astype(jnp.bfloat16)
    rounded = lax.optimization_barrier(rounded)
    return rounded.astype(jnp.float32)


def gamma_adjoint(perambulator):
    order = perambulator.shape[2]
    signs = jnp.where(jnp.arange(order) < order // 2, 1.0, -1.0).astype(jnp.float32)
    both_signs = signs[:, None] * signs[None, :]
    conjugate = jnp.stack([perambulator[:, 0], -perambulator[:, 1]], axis=1)
    return jnp.swapaxes(conjugate, 2, 3) * both_signs


def reference(near_prop, far_prop, meson):
    meson_full = meson.astype(jnp.float32)
    total = jnp.zeros(meson.shape, jnp.float32)
    for separation, perambulator in ((SEP_NEAR, near_prop), (SEP_FAR, far_prop)):
        prop_full = perambulator.astype(jnp.float32)
        adjoint = gamma_adjoint(prop_full)
        shifted = jnp.roll(meson_full, -separation, axis=0)
        ahead = to_half(complex_product(shifted, prop_full))
        total = total + complex_product(adjoint, ahead)
        inner = to_half(complex_product(meson_full, adjoint))
        backward = to_half(complex_product(prop_full, inner))
        total = total + jnp.roll(backward, separation, axis=0)
    return total
```

```python
import functools

import jax
import jax.numpy as jnp
from jax import lax
from jax.experimental import pallas as pl
from jax.experimental.pallas import tpu as pltpu
from jax.sharding import PartitionSpec as P

MESH = pl.DeviceIdType.MESH
BF16 = jnp.bfloat16
F32 = jnp.float32
SENDS = 64
CHUNKS = 2


def kernel(
    n_tm, n_col, near, far, meson, f_home, b_home,
    m_own, m_near, m_far, p_near, p_far, a_near, a_far, inner, b_out, b_in, bx_out, bx_near, bx_far, n_out, s_out, f_sum, f_out,
    m_sem, p_sem, b_sem, bx_sem, f_sem, bh_sem, s_sem,
):
    order = near.shape[2]
    width = near.shape[3]
    half = order // 2
    rows_of = order // CHUNKS
    tm = lax.axis_index("tm")
    me = lax.axis_index("col")
    y, c = me // 2, me % 2
    step_near, step_far = n_tm // 8, 3 * n_tm // 8
    between = step_far - step_near
    odd = lax.rem(tm // step_near, 2)
    partner = 2 * y + 1 - c
    across = 2 * (1 - y) + c
    beyond = 2 * (1 - y) + 1 - c

    def shifted(by):
        return lax.rem(tm + by + n_tm, n_tm)

    barrier = pltpu.get_barrier_semaphore()
    peers = [(tm, partner), (tm, across)]
    for step in (step_near, between):
        for by in (step, -step):
            peers += [(shifted(by), me), (shifted(by), across)]
    for by in (step_far, -step_far):
        peers.append((shifted(by), me))
    for peer in peers:
        pl.semaphore_signal(barrier, inc=1, device_id=peer, device_id_type=MESH)
    pl.semaphore_wait(barrier, len(peers))

    sent = []

    def send(src, dst, recv, device, when=None):
        copy = pltpu.make_async_remote_copy(
            src_ref=src, dst_ref=dst, send_sem=s_sem.at[len(sent)], recv_sem=recv, device_id=device, device_id_type=MESH
        )
        sent.append((copy, when))
        if when is None:
            copy.start()
        else:
            pl.when(when)(copy.start)

    def columns(ref, j):
        return ref.at[:, :, pl.ds(pl.multiple_of(j * width, width), width)]

    def wait(ref, sem):
        pltpu.make_async_copy(ref, ref, sem).wait()

    def arrived(ref, sem, j):
        wait(columns(ref, j), sem.at[j])

    direct = (odd == 1) & (c == 1)
    relays = (odd == 1) | (c == 0)

    def spread_meson(src, j):
        send(src, columns(m_near, j), m_sem.at[1, j], (shifted(-step_near), me))
        send(src, columns(m_far, j), m_sem.at[2, j], (shifted(-step_far), me), direct)

    def to_partner(src, ref, sem, j):
        send(src, columns(ref, j), sem.at[j], (tm, partner))

    operands = ((meson, m_own, m_sem.at[0]), (far, p_far, p_sem.at[1]), (near, p_near, p_sem.at[0]))
    for source, ref, sem in operands:
        send(source.at[1 - y], columns(ref, me), sem.at[me], (tm, across))
        if source is meson:
            spread_meson(meson.at[y], me)
    for source, ref, sem in operands:
        to_partner(source.at[y], ref, sem, me)
        pltpu.make_async_copy(source.at[y], columns(ref, me), sem.at[me]).start()

    def pass_on(ref, sem, j):
        arrived(ref, sem, j)
        to_partner(columns(ref, j), ref, sem, j)

    def relay(j):
        arrived(m_near, m_sem.at[1], j)
        send(columns(m_near, j), columns(m_far, j), m_sem.at[2, j], (shifted(-between), me), relays)
        to_partner(columns(m_near, j), m_near, m_sem.at[1], j)

    rows = lax.broadcasted_iota(jnp.int32, (order, width), 0)

    def adjoint(ref, out, j):
        lanes = lax.broadcasted_iota(jnp.int32, (order, width), 1) + j * width
        sign = jnp.where((rows < half) == (lanes < half), 1.0, -1.0).astype(F32)
        first = pl.multiple_of(j * width, width)
        for part in range(2):
            block = ref[part, :, pl.ds(first, width)].astype(F32) * (sign if part == 0 else -sign)
            out[part, pl.ds(first, width), :] = jnp.transpose(block).astype(BF16)

    def mine(ref):
        picked = []
        for part in range(2):
            for k in range(2):
                picked.append(ref[part, :, pl.ds(pl.multiple_of((2 * k + c) * width, width), width)])
        return jnp.concatenate(picked, axis=1)

    tile = 2 * width

    def product(left, at, right):
        first = jnp.dot(left[0, at, :], right, preferred_element_type=F32)
        second = jnp.dot(left[1, at, :], right, preferred_element_type=F32)
        return first[:, :tile] - second[:, tile:], first[:, tile:] + second[:, :tile]

    def fill_inner(left, right):
        for i in range(CHUNKS):
            at = slice(i * rows_of, (i + 1) * rows_of)
            real, imag = product(left, at, right)
            inner[at, :tile] = real.astype(BF16)
            inner[at, tile:] = imag.astype(BF16)

    def piece(ref, k, i):
        return ref.at[k, :, pl.ds(i * rows_of, rows_of), :]

    relay(me)
    pass_on(m_own, m_sem.at[0], across)
    spread_meson(columns(m_own, across), across)
    for ref, out, sem in ((p_far, a_far, p_sem.at[1]), (p_near, a_near, p_sem.at[0])):
        for j in (me, partner):
            arrived(ref, sem, j)
            adjoint(ref, out, j)
    pass_on(p_far, p_sem.at[1], across)
    adjoint(p_far, a_far, across)
    for j in (me, partner, beyond):
        arrived(m_own, m_sem.at[0], j)
    arrived(p_far, p_sem.at[1], beyond)
    adjoint(p_far, a_far, beyond)

    fill_inner(m_own, mine(a_far))
    for i in range(CHUNKS):
        at = slice(i * rows_of, (i + 1) * rows_of)
        parts = product(p_far, at, inner[...])
        for k in range(2):
            for part in range(2):
                b_out[k, part, at, :] = parts[part][:, k * width:(k + 1) * width].astype(BF16)
            send(piece(b_out, k, i), piece(b_in, k, i), b_sem.at[k, i], (shifted(between), me), jnp.logical_not(direct))
            send(piece(b_out, k, i), piece(bx_far, k, i), bx_sem.at[1, k, i], (shifted(step_near), me), direct)

    relay(across)
    pass_on(p_near, p_sem.at[0], across)
    adjoint(p_near, a_near, across)
    arrived(p_near, p_sem.at[0], beyond)
    adjoint(p_near, a_near, beyond)

    fill_inner(m_own, mine(a_near))
    for i in range(CHUNKS):
        at = slice(i * rows_of, (i + 1) * rows_of)
        parts = product(p_near, at, inner[...])
        for k in range(2):
            for part in range(2):
                n_out[k, part, at, :] = parts[part][:, k * width:(k + 1) * width].astype(BF16)
            send(piece(n_out, k, i), piece(bx_near, k, i), bx_sem.at[0, k, i], (shifted(-step_near), me), direct)

    gathers = (odd == 0) & (c == 1)

    def merge(i):
        for k in range(2):
            @pl.when(jnp.logical_not(direct))
            def _():
                wait(piece(b_in, k, i), b_sem.at[k, i])
                at = pl.ds(i * rows_of, rows_of)
                s_out[k, :, at, :] = (n_out[k, :, at, :].astype(F32) + b_in[k, :, at, :].astype(F32)).astype(BF16)

            send(piece(s_out, k, i), piece(b_home, y, i), bh_sem.at[y, i], (shifted(step_near), 2 * k + c), jnp.logical_not(direct))

            @pl.when(gathers)
            def _():
                wait(piece(bx_near, k, i), bx_sem.at[0, k, i])
                wait(piece(bx_far, k, i), bx_sem.at[1, k, i])
                at = pl.ds(i * rows_of, rows_of)
                bx_out[k, :, at, :] = (bx_near[k, :, at, :].astype(F32) + bx_far[k, :, at, :].astype(F32)).astype(BF16)

            send(piece(bx_out, k, i), piece(b_home, y, i), bh_sem.at[y, i], (shifted(between), 2 * k + c), gathers)

    merge(0)

    for j in (me, across):
        pass_on(m_far, m_sem.at[2], j)
    for j in (partner, beyond):
        arrived(m_near, m_sem.at[1], j)
    fill_inner(m_near, mine(p_near))
    whole = slice(0, order)
    for i in range(CHUNKS):
        at = slice(i * rows_of, (i + 1) * rows_of)
        parts = product(a_near, at, inner[...])
        for part in range(2):
            f_sum[part, at, :] = parts[part]

    for i in range(1, CHUNKS):
        merge(i)

    for j in (partner, beyond):
        arrived(m_far, m_sem.at[2], j)
    fill_inner(m_far, mine(p_far))
    for i in range(CHUNKS):
        at = slice(i * rows_of, (i + 1) * rows_of)
        parts = product(a_far, at, inner[...])
        for k in range(2):
            cut = slice(k * width, (k + 1) * width)
            for part in range(2):
                f_out[k, part, at, :] = (f_sum[part, at, cut] + parts[part][:, cut]).astype(BF16)
    send(f_out.at[1 - y], f_home.at[y], f_sem.at[y], (tm, across))
    pltpu.make_async_copy(f_out.at[y], f_home.at[y], f_sem.at[y]).start()

    for k in range(2):
        wait(f_home.at[k], f_sem.at[k])
        for i in range(CHUNKS):
            wait(piece(b_home, k, i), bh_sem.at[k, i])
    for copy, when in sent:
        if when is None:
            copy.wait_send()
        else:
            pl.when(when)(copy.wait_send)


def shards(n_tm, n_col, near_prop, far_prop, meson):
    slices, parts, order, width = meson.shape
    whole = pltpu.VMEM((parts, order, order), BF16)
    pair = pltpu.VMEM((2, parts, order, width), BF16)
    home = jax.ShapeDtypeStruct((slices, parts, order, width), BF16)
    dma = pltpu.SemaphoreType.DMA
    forward, backward = pl.pallas_call(
        functools.partial(kernel, n_tm, n_col),
        out_shape=(home, home),
        in_specs=[pl.BlockSpec(memory_space=pl.ANY)] * 3,
        out_specs=[pl.BlockSpec(memory_space=pl.ANY)] * 2,
        scratch_shapes=[
            whole, whole, whole, whole, whole, whole, whole,
            pltpu.VMEM((order, 4 * width), BF16),
            pair, pair, pair, pair, pair, pair, pair,
            pltpu.VMEM((parts, order, 2 * width), F32), pair,
            dma((3, n_col)), dma((2, n_col)), dma((2, CHUNKS)), dma((2, 2, CHUNKS)), dma((2,)), dma((2, CHUNKS)), dma((SENDS,)),
        ],
        compiler_params=pltpu.CompilerParams(
            collective_id=0, has_side_effects=True, vmem_limit_bytes=56 * 1024 * 1024
        ),
    )(near_prop, far_prop, meson)
    return forward.astype(F32) + backward.astype(F32)


def solution(mesh):
    spec = P("tm", None, None, "col")
    body = functools.partial(shards, mesh.shape["tm"], mesh.shape["col"])
    return jax.shard_map(body, mesh=mesh, in_specs=(spec, spec, spec), out_specs=spec, check_vma=False)
```

```python
import functools

import jax
import jax.numpy as jnp
from jax import lax
from jax.experimental import pallas as pl
from jax.experimental.pallas import tpu as pltpu
from jax.sharding import PartitionSpec as P

MESH = pl.DeviceIdType.MESH
BF16 = jnp.bfloat16
F32 = jnp.float32
SENDS = 128
CHUNKS = 2
PARTS = 4
ORDER = (
    "up", "m0.2", "m0.0", "adjf1", "m0.1", "m1.me.0", "m1.me.1", "m1.me.2",
    "m1.me.3", "m0.3", "pf", "m1.ac.0", "m1.mep", "m1.ac.1", "adjn1", "m1.ac.2",
    "m0p", "m1.ac.3", "Bf", "pn", "m3.me.1", "m1.acp", "m3.me.2", "m3.me.0",
    "Bn", "m3.me.3", "m3.ac.2", "Fn", "m3.mep", "m3.ac.1", "m3.ac.0", "m3.ac.3",
    "m3.acp", "h1.0.0", "Ff", "h1.1.0", "h2.1.0", "h1.0.1", "h2.0.0", "h2.0.1",
    "h1.1.1", "h2.1.1",
)


def kernel(
    n_tm, n_col, near, far, meson, f_home, b_home,
    m_own, m_near, m_far, p_near, p_far, a_near, a_far, inner, b_out, b_in, bx_out, bx_near, bx_far, n_out, s_out, f_sum, f_out,
    m_sem, p_sem, b_sem, bx_sem, f_sem, bh_sem, s_sem, ready,
):
    order = near.shape[2]
    width = near.shape[3]
    half = order // 2
    tile = 2 * width
    tm = lax.axis_index("tm")
    me = lax.axis_index("col")
    y, c = me // 2, me % 2
    step_near, step_far = n_tm // 8, 3 * n_tm // 8
    between = step_far - step_near
    place = tm // step_near
    odd = lax.rem(place, 2)
    partner = 2 * y + 1 - c
    across = 2 * (1 - y) + c
    beyond = 2 * (1 - y) + 1 - c

    def shifted(by):
        return lax.rem(tm + by + n_tm, n_tm)

    def above(by):
        return lax.rem(place + by + 8, 8) > place

    barrier = pltpu.get_barrier_semaphore()
    reach = (1, -1, 2, -2, 3, -3)
    for peer in (partner, across):
        pl.semaphore_signal(barrier, inc=1, device_id=(tm, peer), device_id_type=MESH)
    later = 0
    for by in reach:
        later = later + 2 * above(by).astype(jnp.int32)
        for peer in (me, across):
            @pl.when(above(by))
            def _():
                pl.semaphore_signal(barrier, inc=1, device_id=(shifted(by * step_near), peer), device_id_type=MESH)
    pl.semaphore_wait(barrier, 2 + 2 * len(reach) - later)
    for by in reach:
        for peer in (me, across):
            @pl.when(jnp.logical_not(above(by)))
            def _():
                pl.semaphore_signal(ready, inc=1, device_id=(shifted(by * step_near), peer), device_id_type=MESH)

    sent = []

    def send(src, dst, recv, device, when=None):
        copy = pltpu.make_async_remote_copy(
            src_ref=src, dst_ref=dst, send_sem=s_sem.at[len(sent)], recv_sem=recv, device_id=device, device_id_type=MESH
        )
        sent.append((copy, when))
        if when is None:
            copy.start()
        else:
            pl.when(when)(copy.start)

    def columns(ref, j):
        return ref.at[:, :, pl.ds(pl.multiple_of(j * width, width), width)]

    def wait(ref, sem):
        pltpu.make_async_copy(ref, ref, sem).wait()

    fine = order // PARTS
    rows_of = order // CHUNKS
    mesons = (m_own, m_near, m_far)

    def part_of(ref, j, i):
        return ref.at[:, pl.ds(i * fine, fine), pl.ds(pl.multiple_of(j * width, width), width)]

    direct = (odd == 1) & (c == 1)
    relays = (odd == 1) | (c == 0)
    gathers = (odd == 0) & (c == 1)

    def spread(src, j, i, when_near, when_far):
        send(src, part_of(m_near, j, i), m_sem.at[1, j, i], (shifted(-step_near), me), when_near)
        send(src, part_of(m_far, j, i), m_sem.at[2, j, i], (shifted(-step_far), me), when_far)

    def own(i):
        return meson.at[y, :, pl.ds(i * fine, fine), :]

    def local(src, dst, sem):
        pltpu.make_async_copy(src, dst, sem).start()

    for i in range(PARTS):
        send(meson.at[1 - y, :, pl.ds(i * fine, fine), :], part_of(m_own, me, i), m_sem.at[0, me, i], (tm, across))
    for i in range(PARTS):
        spread(own(i), me, i, jnp.logical_not(above(-1)), direct & jnp.logical_not(above(-3)))
    send(far.at[1 - y], columns(p_far, me), p_sem.at[1, me], (tm, across))
    send(near.at[1 - y], columns(p_near, me), p_sem.at[0, me], (tm, across))
    for src, ref, sem in ((meson, m_own, m_sem.at[0, me, 0]), (far, p_far, p_sem.at[1, me]), (near, p_near, p_sem.at[0, me])):
        send(src.at[y], columns(ref, me), sem, (tm, partner))
        local(src.at[y], columns(ref, me), sem)

    rows = lax.broadcasted_iota(jnp.int32, (order, width), 0)

    def adjoint(ref, out, j):
        lanes = lax.broadcasted_iota(jnp.int32, (order, width), 1) + j * width
        sign = jnp.where((rows < half) == (lanes < half), 1.0, -1.0).astype(F32)
        first = pl.multiple_of(j * width, width)
        for part in range(2):
            block = ref[part, :, pl.ds(first, width)].astype(F32) * (sign if part == 0 else -sign)
            out[part, pl.ds(first, width), :] = jnp.transpose(block).astype(BF16)

    def mine(ref):
        picked = []
        for part in range(2):
            for k in range(2):
                picked.append(ref[part, :, pl.ds(pl.multiple_of((2 * k + c) * width, width), width)])
        return jnp.concatenate(picked, axis=1)

    def product(left, at, right):
        first = jnp.dot(left[0, at, :], right, preferred_element_type=F32)
        second = jnp.dot(left[1, at, :], right, preferred_element_type=F32)
        return first[:, :tile] - second[:, tile:], first[:, tile:] + second[:, :tile]

    def fill_inner(left, right):
        for i in range(CHUNKS):
            at = slice(i * rows_of, (i + 1) * rows_of)
            real, imag = product(left, at, right)
            inner[at, :tile] = real.astype(BF16)
            inner[at, tile:] = imag.astype(BF16)

    def piece(ref, k, i):
        return ref.at[k, :, pl.ds(i * rows_of, rows_of), :]

    def whole_meson(which):
        for j in (partner, beyond):
            wait(columns(mesons[which], j), m_sem.at[which, j, 0])

    def store(out, parts, at):
        for k in range(2):
            for part in range(2):
                out[k, part, at, :] = parts[part][:, k * width:(k + 1) * width].astype(BF16)

    def run(step):
        name, *rest = step.split(".")
        if name == "up":
            @pl.when(later > 0)
            def _():
                pl.semaphore_wait(ready, later)

            for i in range(PARTS):
                spread(own(i), me, i, above(-1), direct & above(-3))
        elif name == "m0":
            i = int(rest[0])
            wait(part_of(m_own, across, i), m_sem.at[0, across, i])
            spread(part_of(m_own, across, i), across, i, None, direct)
        elif name == "m0p":
            send(columns(m_own, across), columns(m_own, across), m_sem.at[0, across, 0], (tm, partner))
        elif name in ("m1", "m3"):
            which = 1 if name == "m1" else 2
            ref, j = mesons[which], me if rest[0].startswith("me") else across
            if rest[0].endswith("p"):
                send(columns(ref, j), columns(ref, j), m_sem.at[which, j, 0], (tm, partner))
                return
            i = int(rest[1])
            wait(part_of(ref, j, i), m_sem.at[which, j, i])
            if which == 1:
                send(part_of(ref, j, i), part_of(m_far, j, i), m_sem.at[2, j, i], (shifted(-between), me), relays)
        elif name in ("adjf1", "adjn1"):
            s, ref, out = (1, p_far, a_far) if name == "adjf1" else (0, p_near, a_near)
            for j in (me, partner):
                wait(columns(ref, j), p_sem.at[s, j])
                adjoint(ref, out, j)
        elif name in ("pf", "pn"):
            s, ref, out = (1, p_far, a_far) if name == "pf" else (0, p_near, a_near)
            wait(columns(ref, across), p_sem.at[s, across])
            send(columns(ref, across), columns(ref, across), p_sem.at[s, across], (tm, partner))
            adjoint(ref, out, across)
        elif name in ("Bf", "Bn"):
            s, ref, adj = (1, p_far, a_far) if name == "Bf" else (0, p_near, a_near)
            if name == first_backward:
                wait(columns(m_own, me), m_sem.at[0, me, 0])
                whole_meson(0)
            wait(columns(ref, beyond), p_sem.at[s, beyond])
            adjoint(ref, adj, beyond)
            fill_inner(m_own, mine(adj))
            for i in range(CHUNKS):
                at = slice(i * rows_of, (i + 1) * rows_of)
                out = b_out if s else n_out
                store(out, product(ref, at, inner[...]), at)
                for k in range(2):
                    if s:
                        send(piece(out, k, i), piece(b_in, k, i), b_sem.at[k, i], (shifted(between), me), jnp.logical_not(direct))
                        send(piece(out, k, i), piece(bx_far, k, i), bx_sem.at[1, k, i], (shifted(step_near), me), direct)
                    else:
                        send(piece(out, k, i), piece(bx_near, k, i), bx_sem.at[0, k, i], (shifted(-step_near), me), direct)
        elif name == "Fn":
            whole_meson(1)
            fill_inner(m_near, mine(p_near))
            for i in range(CHUNKS):
                at = slice(i * rows_of, (i + 1) * rows_of)
                parts = product(a_near, at, inner[...])
                for part in range(2):
                    f_sum[part, at, :] = parts[part]
        elif name == "Ff":
            whole_meson(2)
            fill_inner(m_far, mine(p_far))
            for i in range(CHUNKS):
                at = slice(i * rows_of, (i + 1) * rows_of)
                parts = product(a_far, at, inner[...])
                store(f_out, (parts[0] + f_sum[0, at, :], parts[1] + f_sum[1, at, :]), at)
            send(f_out.at[1 - y], f_home.at[y], f_sem.at[y], (tm, across))
            local(f_out.at[y], f_home.at[y], f_sem.at[y])
        elif name in ("h1", "h2"):
            k, i = int(rest[0]), int(rest[1])
            at = pl.ds(i * rows_of, rows_of)
            if name == "h1":
                when, out, by = jnp.logical_not(direct), s_out, step_near

                @pl.when(when)
                def _():
                    wait(piece(b_in, k, i), b_sem.at[k, i])
                    s_out[k, :, at, :] = (n_out[k, :, at, :].astype(F32) + b_in[k, :, at, :].astype(F32)).astype(BF16)
            else:
                when, out, by = gathers, bx_out, between

                @pl.when(when)
                def _():
                    wait(piece(bx_near, k, i), bx_sem.at[0, k, i])
                    wait(piece(bx_far, k, i), bx_sem.at[1, k, i])
                    bx_out[k, :, at, :] = (bx_near[k, :, at, :].astype(F32) + bx_far[k, :, at, :].astype(F32)).astype(BF16)

            send(piece(out, k, i), piece(b_home, y, i), bh_sem.at[y, i], (shifted(by), 2 * k + c), when)

    first_backward = min(("Bf", "Bn"), key=ORDER.index)
    for step in ORDER:
        run(step)

    for k in range(2):
        wait(f_home.at[k], f_sem.at[k])
        for i in range(CHUNKS):
            wait(piece(b_home, k, i), bh_sem.at[k, i])
    for copy, when in sent:
        if when is None:
            copy.wait_send()
        else:
            pl.when(when)(copy.wait_send)


def shards(n_tm, n_col, near_prop, far_prop, meson):
    slices, parts, order, width = meson.shape
    whole = pltpu.VMEM((parts, order, order), BF16)
    pair = pltpu.VMEM((2, parts, order, width), BF16)
    home = jax.ShapeDtypeStruct((slices, parts, order, width), BF16)
    dma = pltpu.SemaphoreType.DMA
    forward, backward = pl.pallas_call(
        functools.partial(kernel, n_tm, n_col),
        out_shape=(home, home),
        in_specs=[pl.BlockSpec(memory_space=pl.ANY)] * 3,
        out_specs=[pl.BlockSpec(memory_space=pl.ANY)] * 2,
        scratch_shapes=[
            whole, whole, whole, whole, whole, whole, whole,
            pltpu.VMEM((order, 4 * width), BF16),
            pair, pair, pair, pair, pair, pair, pair,
            pltpu.VMEM((parts, order, 2 * width), F32), pair,
            dma((3, n_col, PARTS)), dma((2, n_col)), dma((2, CHUNKS)), dma((2, 2, CHUNKS)), dma((2,)), dma((2, CHUNKS)), dma((SENDS,)),
            pltpu.SemaphoreType.REGULAR,
        ],
        compiler_params=pltpu.CompilerParams(
            collective_id=0, has_side_effects=True, vmem_limit_bytes=56 * 1024 * 1024
        ),
    )(near_prop, far_prop, meson)
    return forward.astype(F32) + backward.astype(F32)


def solution(mesh):
    spec = P("tm", None, None, "col")
    body = functools.partial(shards, mesh.shape["tm"], mesh.shape["col"])
    return jax.shard_map(body, mesh=mesh, in_specs=(spec, spec, spec), out_specs=spec, check_vma=False)
```

```python
import functools

import jax
import jax.numpy as jnp
from jax import lax
from jax.experimental import pallas as pl
from jax.experimental.pallas import tpu as pltpu
from jax.sharding import PartitionSpec as P

MESH = pl.DeviceIdType.MESH
BF16 = jnp.bfloat16
F32 = jnp.float32
SENDS = 256
CHUNKS = 2
PARTS = 4
ORDER = (
    "adjf1", "up", "m0.0", "m0.2", "m1.me.0", "m1.me.1", "m1.me.2", "m0.3",
    "m0.1", "m1.me.3", "m3.me.0", "m1.mep", "adjn1", "m1.ac.0", "pf", "m0p",
    "m1.ac.3", "m3.me.2", "m1.ac.2", "m1.ac.1", "Bf", "pn", "m3.ac.0", "m3.me.3",
    "m3.me.1", "m3.mep", "m1.acp", "Bn", "Fn", "m3.ac.1", "m3.ac.2", "m3.ac.3",
    "m3.acp", "Ff", "h1.0.0", "h2.0.0", "h2.1.0", "h1.1.0", "h2.0.1", "h1.0.1",
    "h2.1.1", "h1.1.1",
)
ISSUE = ('m', 's', 'f', 'n')
MESON_ROUTES = {
    (0, 0): ((0, 7), (7, 5),),
    (0, 1): ((0, 7), (7, 5),),
    (1, 0): ((0, 6), (1, 0),),
    (1, 1): ((1, 0), (1, 6),),
    (2, 0): ((1, 7), (2, 1),),
    (2, 1): ((1, 7), (2, 1),),
    (3, 0): ((2, 0), (3, 2),),
    (3, 1): ((3, 0), (3, 2),),
    (4, 0): ((3, 1), (4, 3),),
    (4, 1): ((3, 1), (4, 3),),
    (5, 0): ((4, 2), (5, 4),),
    (5, 1): ((5, 2), (5, 4),),
    (6, 0): ((5, 3), (6, 5),),
    (6, 1): ((5, 3), (6, 5),),
    (7, 0): ((6, 4), (7, 6),),
    (7, 1): ((7, 4), (7, 6),),
}
SUM_ROUTES = {
    (0, 0): ((5, 7), (7, 0),),
    (0, 1): ((5, 6), (6, 0), (7, 6),),
    (1, 0): ((0, 1), (6, 0),),
    (1, 1): ((0, 1), (6, 0),),
    (2, 0): ((1, 2), (7, 1),),
    (2, 1): ((0, 2), (1, 0), (7, 0),),
    (3, 0): ((0, 2), (2, 3),),
    (3, 1): ((0, 2), (2, 3),),
    (4, 0): ((1, 3), (3, 4),),
    (4, 1): ((1, 2), (2, 4), (3, 2),),
    (5, 0): ((2, 4), (4, 5),),
    (5, 1): ((2, 4), (4, 5),),
    (6, 0): ((3, 5), (5, 6),),
    (6, 1): ((3, 4), (4, 6), (5, 4),),
    (7, 0): ((4, 6), (6, 7),),
    (7, 1): ((4, 6), (6, 7),),
}


def short(by):
    by %= 8
    return by - 8 if by > 4 else by


def table(routes):
    masks = {}
    for (goal, core), edges in routes.items():
        for source, target in edges:
            key = ((goal - source) % 8, short(target - source))
            masks[key] = masks.get(key, 0) | 1 << 2 * source + core
    return dict(sorted(masks.items()))


MESON_SENDS = table(MESON_ROUTES)
SUM_SENDS = table(SUM_ROUTES)
REACH = sorted({by * way for _, by in (*MESON_SENDS, *SUM_SENDS) for way in (1, -1) if abs(by) < 4} | {by for _, by in (*MESON_SENDS, *SUM_SENDS) if by == 4})


def sum_inputs():
    found = {}
    for (goal, core), edges in SUM_ROUTES.items():
        for place in range(8):
            gap = (goal - place) % 8
            inputs = tuple(sorted(short(source - target) for source, target in edges if target == place))
            if gap and inputs:
                found[gap, inputs] = found.get((gap, inputs), 0) | 1 << 2 * place + core
    return dict(sorted(found.items()))


SUM_INPUTS = sum_inputs()
LANDINGS = sorted({(gap, by) for gap, inputs in SUM_INPUTS for by in inputs})
SUMS = sorted({gap for gap, _ in SUM_INPUTS})
EXTRA = sorted({(gap - by) % 8 for gap, by in MESON_SENDS} - {0, 1, 3})


def kernel(
    n_tm, n_col, near, far, meson, f_home, b_home,
    m_own, m_near, m_far, m_extra, p_near, p_far, a_near, a_far, inner, b_out, n_out, landing, sums, f_sum, f_out,
    m_sem, p_sem, b_sem, f_sem, bh_sem, s_sem, ready,
):
    order = near.shape[2]
    width = near.shape[3]
    half = order // 2
    tile = 2 * width
    tm = lax.axis_index("tm")
    me = lax.axis_index("col")
    y, c = me // 2, me % 2
    stride = n_tm // 8
    place = tm // stride
    partner = 2 * y + 1 - c
    across = 2 * (1 - y) + c
    beyond = 2 * (1 - y) + 1 - c

    def shifted(by):
        return lax.rem(tm + by * stride + n_tm, n_tm)

    def among(mask):
        return lax.rem(lax.shift_right_logical(jnp.int32(mask), 2 * place + c), 2) == 1

    def above(by):
        return lax.rem(place + by + 8, 8) > place

    barrier = pltpu.get_barrier_semaphore()
    for peer in (partner, across):
        pl.semaphore_signal(barrier, inc=1, device_id=(tm, peer), device_id_type=MESH)
    later = 0
    for by in REACH:
        later = later + 2 * above(by).astype(jnp.int32)
        for peer in (me, across):
            @pl.when(above(by))
            def _():
                pl.semaphore_signal(barrier, inc=1, device_id=(shifted(by), peer), device_id_type=MESH)
    pl.semaphore_wait(barrier, 2 + 2 * len(REACH) - later)
    for by in REACH:
        for peer in (me, across):
            @pl.when(jnp.logical_not(above(by)))
            def _():
                pl.semaphore_signal(ready, inc=1, device_id=(shifted(by), peer), device_id_type=MESH)

    sent = []

    def send(src, dst, recv, device, when=None):
        copy = pltpu.make_async_remote_copy(
            src_ref=src, dst_ref=dst, send_sem=s_sem.at[len(sent)], recv_sem=recv, device_id=device, device_id_type=MESH
        )
        sent.append((copy, when))
        if when is None:
            copy.start()
        else:
            pl.when(when)(copy.start)

    def columns(ref, j):
        return ref.at[:, :, pl.ds(pl.multiple_of(j * width, width), width)]

    def wait(ref, sem):
        pltpu.make_async_copy(ref, ref, sem).wait()

    fine = order // PARTS
    rows_of = order // CHUNKS
    mesons = {0: m_own, 1: m_near, 3: m_far, **{gap: m_extra.at[n] for n, gap in enumerate(EXTRA)}}

    def part_of(ref, j, i):
        return ref.at[:, pl.ds(i * fine, fine), pl.ds(pl.multiple_of(j * width, width), width)]

    def spread(src, gap, j, i, some=None):
        for (start, by), mask in MESON_SENDS.items():
            if start == gap:
                to = (gap - by) % 8
                when = among(mask) if some is None else among(mask) & some(by)
                send(src, part_of(mesons[to], j, i), m_sem.at[to, j, i], (shifted(by), me), when)

    def own(i):
        return meson.at[y, :, pl.ds(i * fine, fine), :]

    def local(src, dst, sem):
        pltpu.make_async_copy(src, dst, sem).start()

    for what in ISSUE:
        if what == "m":
            for i in range(PARTS):
                src = meson.at[1 - y, :, pl.ds(i * fine, fine), :]
                send(src, part_of(m_own, me, i), m_sem.at[0, me, i], (tm, across))
        elif what == "s":
            for i in range(PARTS):
                spread(own(i), 0, me, i, lambda by: jnp.logical_not(above(by)))
        elif what == "f":
            send(far.at[1 - y], columns(p_far, me), p_sem.at[1, me], (tm, across))
        else:
            send(near.at[1 - y], columns(p_near, me), p_sem.at[0, me], (tm, across))
    for src, ref, sem in ((meson, m_own, m_sem.at[0, me, 0]), (far, p_far, p_sem.at[1, me]), (near, p_near, p_sem.at[0, me])):
        send(src.at[y], columns(ref, me), sem, (tm, partner))
        local(src.at[y], columns(ref, me), sem)

    rows = lax.broadcasted_iota(jnp.int32, (order, width), 0)

    def adjoint(ref, out, j):
        lanes = lax.broadcasted_iota(jnp.int32, (order, width), 1) + j * width
        sign = jnp.where((rows < half) == (lanes < half), 1.0, -1.0).astype(F32)
        first = pl.multiple_of(j * width, width)
        for part in range(2):
            block = ref[part, :, pl.ds(first, width)].astype(F32) * (sign if part == 0 else -sign)
            out[part, pl.ds(first, width), :] = jnp.transpose(block).astype(BF16)

    def mine(ref):
        picked = []
        for part in range(2):
            for k in range(2):
                picked.append(ref[part, :, pl.ds(pl.multiple_of((2 * k + c) * width, width), width)])
        return jnp.concatenate(picked, axis=1)

    def product(left, at, right):
        first = jnp.dot(left[0, at, :], right, preferred_element_type=F32)
        second = jnp.dot(left[1, at, :], right, preferred_element_type=F32)
        return first[:, :tile] - second[:, tile:], first[:, tile:] + second[:, :tile]

    def fill_inner(left, right):
        for i in range(CHUNKS):
            at = slice(i * rows_of, (i + 1) * rows_of)
            real, imag = product(left, at, right)
            inner[at, :tile] = real.astype(BF16)
            inner[at, tile:] = imag.astype(BF16)

    def piece(ref, k, i):
        return ref.at[k, :, pl.ds(i * rows_of, rows_of), :]

    def whole_meson(gap):
        for j in (partner, beyond):
            wait(columns(mesons[gap], j), m_sem.at[gap, j, 0])

    def store(out, parts, at):
        for k in range(2):
            for part in range(2):
                out[k, part, at, :] = parts[part][:, k * width:(k + 1) * width].astype(BF16)

    def run(step):
        name, *rest = step.split(".")
        if name == "up":
            @pl.when(later > 0)
            def _():
                pl.semaphore_wait(ready, later)

            for i in range(PARTS):
                spread(own(i), 0, me, i, above)
        elif name == "m0":
            i = int(rest[0])
            wait(part_of(m_own, across, i), m_sem.at[0, across, i])
            spread(part_of(m_own, across, i), 0, across, i)
        elif name == "m0p":
            send(columns(m_own, across), columns(m_own, across), m_sem.at[0, across, 0], (tm, partner))
        elif name[0] == "m":
            gap = int(name[1:])
            ref, j = mesons[gap], me if rest[0].startswith("me") else across
            if rest[0].endswith("p"):
                send(columns(ref, j), columns(ref, j), m_sem.at[gap, j, 0], (tm, partner))
                return
            i = int(rest[1])
            arrivals = 0
            for (start, by), mask in MESON_SENDS.items():
                if (start - by) % 8 == gap:
                    for bit in range(16):
                        if mask >> bit & 1:
                            arrivals |= 1 << (bit + 2 * by) % 16

            @pl.when(among(arrivals))
            def _():
                wait(part_of(ref, j, i), m_sem.at[gap, j, i])

            spread(part_of(ref, j, i), gap, j, i)
        elif name in ("adjf1", "adjn1"):
            s, ref, out = (1, p_far, a_far) if name == "adjf1" else (0, p_near, a_near)
            for j in (me, partner):
                wait(columns(ref, j), p_sem.at[s, j])
                adjoint(ref, out, j)
        elif name in ("pf", "pn"):
            s, ref, out = (1, p_far, a_far) if name == "pf" else (0, p_near, a_near)
            wait(columns(ref, across), p_sem.at[s, across])
            send(columns(ref, across), columns(ref, across), p_sem.at[s, across], (tm, partner))
            adjoint(ref, out, across)
        elif name in ("Bf", "Bn"):
            s, ref, adj = (1, p_far, a_far) if name == "Bf" else (0, p_near, a_near)
            if name == first_backward:
                wait(columns(m_own, me), m_sem.at[0, me, 0])
                whole_meson(0)
            wait(columns(ref, beyond), p_sem.at[s, beyond])
            adjoint(ref, adj, beyond)
            fill_inner(m_own, mine(adj))
            for i in range(CHUNKS):
                at = slice(i * rows_of, (i + 1) * rows_of)
                out = b_out if s else n_out
                store(out, product(ref, at, inner[...]), at)
                for k in range(2):
                    pass_sum(out, 3 if s else 1, k, i, False)
        elif name == "Fn":
            whole_meson(1)
            fill_inner(m_near, mine(p_near))
            for i in range(CHUNKS):
                at = slice(i * rows_of, (i + 1) * rows_of)
                parts = product(a_near, at, inner[...])
                for part in range(2):
                    f_sum[part, at, :] = parts[part]
        elif name == "Ff":
            whole_meson(3)
            fill_inner(m_far, mine(p_far))
            for i in range(CHUNKS):
                at = slice(i * rows_of, (i + 1) * rows_of)
                parts = product(a_far, at, inner[...])
                store(f_out, (parts[0] + f_sum[0, at, :], parts[1] + f_sum[1, at, :]), at)
            send(f_out.at[1 - y], f_home.at[y], f_sem.at[y], (tm, across))
            local(f_out.at[y], f_home.at[y], f_sem.at[y])
        elif name[0] == "h":
            gap, k, i = int(name[1:]), int(rest[0]), int(rest[1])
            at = pl.ds(i * rows_of, rows_of)
            out = sums.at[SUMS.index(gap)]
            mine_too = {1: n_out, 3: b_out}.get(gap)
            for (start, inputs), mask in SUM_INPUTS.items():
                if start == gap:
                    @pl.when(among(mask))
                    def _():
                        terms = [] if mine_too is None else [mine_too[k, :, at, :].astype(F32)]
                        for by in inputs:
                            slot = LANDINGS.index((gap, by))
                            wait(piece(landing.at[slot], k, i), b_sem.at[slot, k, i])
                            terms.append(landing[slot, k, :, at, :].astype(F32))
                        out[k, :, at, :] = functools.reduce(jnp.add, terms).astype(BF16)

            pass_sum(out, gap, k, i, True)

    def pass_sum(src, gap, k, i, summed):
        summing = 0
        for (start, _), mask in SUM_INPUTS.items():
            if start == gap:
                summing |= mask
        for (start, by), mask in SUM_SENDS.items():
            mask &= summing if summed else ~summing
            if start != gap or not mask:
                continue
            if by == short(gap):
                send(piece(src, k, i), piece(b_home, y, i), bh_sem.at[y, i], (shifted(by), 2 * k + c), among(mask))
            else:
                slot = LANDINGS.index(((gap - by) % 8, short(-by)))
                send(piece(src, k, i), piece(landing.at[slot], k, i), b_sem.at[slot, k, i], (shifted(by), me), among(mask))

    first_backward = min(("Bf", "Bn"), key=ORDER.index)
    for step in ORDER:
        run(step)

    for k in range(2):
        wait(f_home.at[k], f_sem.at[k])
        for i in range(CHUNKS):
            wait(piece(b_home, k, i), bh_sem.at[k, i])
    for copy, when in sent:
        if when is None:
            copy.wait_send()
        else:
            pl.when(when)(copy.wait_send)


def shards(n_tm, n_col, near_prop, far_prop, meson):
    slices, parts, order, width = meson.shape
    whole = pltpu.VMEM((parts, order, order), BF16)
    pair = pltpu.VMEM((2, parts, order, width), BF16)
    home = jax.ShapeDtypeStruct((slices, parts, order, width), BF16)
    dma = pltpu.SemaphoreType.DMA
    forward, backward = pl.pallas_call(
        functools.partial(kernel, n_tm, n_col),
        out_shape=(home, home),
        in_specs=[pl.BlockSpec(memory_space=pl.ANY)] * 3,
        out_specs=[pl.BlockSpec(memory_space=pl.ANY)] * 2,
        scratch_shapes=[
            whole, whole, whole, pltpu.VMEM((max(1, len(EXTRA)), parts, order, order), BF16), whole, whole, whole, whole,
            pltpu.VMEM((order, 4 * width), BF16),
            pair, pair, pltpu.VMEM((len(LANDINGS), *pair.shape), BF16), pltpu.VMEM((len(SUMS), *pair.shape), BF16),
            pltpu.VMEM((parts, order, 2 * width), F32), pair,
            dma((8, n_col, PARTS)), dma((2, n_col)), dma((len(LANDINGS), 2, CHUNKS)), dma((2,)), dma((2, CHUNKS)), dma((SENDS,)),
            pltpu.SemaphoreType.REGULAR,
        ],
        compiler_params=pltpu.CompilerParams(
            collective_id=0, has_side_effects=True, vmem_limit_bytes=56 * 1024 * 1024
        ),
    )(near_prop, far_prop, meson)
    return forward.astype(F32) + backward.astype(F32)


def solution(mesh):
    spec = P("tm", None, None, "col")
    body = functools.partial(shards, mesh.shape["tm"], mesh.shape["col"])
    return jax.shard_map(body, mesh=mesh, in_specs=(spec, spec, spec), out_specs=spec, check_vma=False)
```

```python
import functools

import jax
import jax.numpy as jnp
from jax import lax
from jax.experimental import pallas as pl
from jax.experimental.pallas import tpu as pltpu
from jax.sharding import PartitionSpec as P

MESH = pl.DeviceIdType.MESH
BF16 = jnp.bfloat16
F32 = jnp.float32
SENDS = 28
EVERY = ()
CHUNKS = 2
PARTS = 4
ORDER = (
    "up", "m0.2", "m0.0", "m1.me.1", "m1.me.2", "m1.me.3", "adjf1", "m0.1",
    "m1.me.0", "m0.3", "pf", "m1.ac.0", "m1.mep", "m1.ac.1", "adjn1", "m1.ac.2",
    "m0p", "m1.ac.3", "Bf", "pn", "m1.acp", "Bn", "Fn", "m3.mep",
    "m3.acp", "h1.0.0", "Ff", "h1.1.0", "drain", "h1.0.1", "h2.0.0", "h1.1.1",
    "h2.1.0", "h2.0.1", "h2.1.1",
)


def kernel(
    n_tm, n_col, near, far, meson, f_home, b_home,
    m_own, m_near, m_far, p_near, p_far, a_near, a_far, inner, b_out, b_in, bx_out, bx_near, bx_far, n_out, s_out, f_sum, f_out,
    m_sem, p_sem, b_sem, bx_sem, f_sem, bh_sem, s_sem, ready,
):
    order = near.shape[2]
    width = near.shape[3]
    half = order // 2
    tile = 2 * width
    tm = lax.axis_index("tm")
    me = lax.axis_index("col")
    y, c = me // 2, me % 2
    step_near, step_far = n_tm // 8, 3 * n_tm // 8
    between = step_far - step_near
    place = tm // step_near
    odd = lax.rem(place, 2)
    partner = 2 * y + 1 - c
    across = 2 * (1 - y) + c
    beyond = 2 * (1 - y) + 1 - c

    def shifted(by):
        return lax.rem(tm + by + n_tm, n_tm)

    def above(by):
        return lax.rem(place + by + 8, 8) > place

    barrier = pltpu.get_barrier_semaphore()
    reach = (1, -1, 2, -2, 3, -3)
    for peer in (partner, across):
        pl.semaphore_signal(barrier, inc=1, device_id=(tm, peer), device_id_type=MESH)
    later = 0
    for by in reach:
        later = later + 2 * above(by).astype(jnp.int32)
        for peer in (me, across):
            @pl.when(above(by))
            def _():
                pl.semaphore_signal(barrier, inc=1, device_id=(shifted(by * step_near), peer), device_id_type=MESH)
    pl.semaphore_wait(barrier, 2 + 2 * len(reach) - later)
    for by in reach:
        for peer in (me, across):
            @pl.when(jnp.logical_not(above(by)))
            def _():
                pl.semaphore_signal(ready, inc=1, device_id=(shifted(by * step_near), peer), device_id_type=MESH)

    groups = {}

    def send(src, dst, recv, device, when=None, group=None, whole=None, waited=None):
        group = len(groups) if group is None else group
        waited = None if waited is EVERY else when if waited is None else waited
        if group not in groups:
            groups[group] = (len(groups), src if whole is None else whole, waited)
        copy = pltpu.make_async_remote_copy(
            src_ref=src, dst_ref=dst, send_sem=s_sem.at[groups[group][0]], recv_sem=recv, device_id=device, device_id_type=MESH
        )
        if when is None:
            copy.start()
        else:
            pl.when(when)(copy.start)

    drained = set()

    def drain(early):
        for group, (n, whole, when) in groups.items():
            if group not in drained and not (early and group in ("h1", "h2")):
                drained.add(group)
                only = pl.when(when) if when is not None else lambda f: f()
                only(pltpu.make_async_copy(whole, whole, s_sem.at[n]).wait)

    def columns(ref, j):
        return ref.at[:, :, pl.ds(pl.multiple_of(j * width, width), width)]

    def wait(ref, sem):
        pltpu.make_async_copy(ref, ref, sem).wait()

    fine = order // PARTS
    rows_of = order // CHUNKS
    mesons = (m_own, m_near, m_far)

    def part_of(ref, j, i):
        return ref.at[:, pl.ds(i * fine, fine), pl.ds(pl.multiple_of(j * width, width), width)]

    direct = (odd == 1) & (c == 1)
    relays = (odd == 1) | (c == 0)
    gathers = (odd == 0) & (c == 1)
    not_direct = jnp.logical_not(direct)

    def spread(src, whole, j, i, when_near, when_far):
        send(src, part_of(m_near, j, i), near_sem(j, i), (shifted(-step_near), me), when_near, ("near", j is me), whole, EVERY)
        send(src, part_of(m_far, j, i), far_sem(j), (shifted(-step_far), me), when_far, ("direct", j is me), whole, direct)

    def own_sem(i):
        return m_sem.at[i]

    def block_sem(which, j):
        return m_sem.at[PARTS + 2 * PARTS + which * n_col + j]

    def near_sem(j, i):
        return m_sem.at[PARTS + (0 if j is me else PARTS) + i]

    def far_sem(j):
        return block_sem(2, j)

    def own(i):
        return meson.at[y, :, pl.ds(i * fine, fine), :]

    def local(src, dst, sem):
        pltpu.make_async_copy(src, dst, sem).start()

    for i in range(PARTS):
        src = meson.at[1 - y, :, pl.ds(i * fine, fine), :]
        send(src, part_of(m_own, me, i), own_sem(i), (tm, across), None, "own", meson.at[1 - y])
    for i in range(PARTS):
        spread(own(i), meson.at[y], me, i, jnp.logical_not(above(-1)), direct & jnp.logical_not(above(-3)))
    send(far.at[1 - y], columns(p_far, me), p_sem.at[1, me], (tm, across))
    send(near.at[1 - y], columns(p_near, me), p_sem.at[0, me], (tm, across))
    for src, ref, sem in ((meson, m_own, block_sem(0, me)), (far, p_far, p_sem.at[1, me]), (near, p_near, p_sem.at[0, me])):
        send(src.at[y], columns(ref, me), sem, (tm, partner))
        local(src.at[y], columns(ref, me), sem)

    rows = lax.broadcasted_iota(jnp.int32, (order, width), 0)

    def adjoint(ref, out, j):
        lanes = lax.broadcasted_iota(jnp.int32, (order, width), 1) + j * width
        sign = jnp.where((rows < half) == (lanes < half), 1.0, -1.0).astype(F32)
        first = pl.multiple_of(j * width, width)
        for part in range(2):
            block = ref[part, :, pl.ds(first, width)].astype(F32) * (sign if part == 0 else -sign)
            out[part, pl.ds(first, width), :] = jnp.transpose(block).astype(BF16)

    def mine(ref):
        picked = []
        for part in range(2):
            for k in range(2):
                picked.append(ref[part, :, pl.ds(pl.multiple_of((2 * k + c) * width, width), width)])
        return jnp.concatenate(picked, axis=1)

    def product(left, at, right):
        first = jnp.dot(left[0, at, :], right, preferred_element_type=F32)
        second = jnp.dot(left[1, at, :], right, preferred_element_type=F32)
        return first[:, :tile] - second[:, tile:], first[:, tile:] + second[:, :tile]

    def fill_inner(left, right):
        for i in range(CHUNKS):
            at = slice(i * rows_of, (i + 1) * rows_of)
            real, imag = product(left, at, right)
            inner[at, :tile] = real.astype(BF16)
            inner[at, tile:] = imag.astype(BF16)

    def piece(ref, k, i):
        return ref.at[k, :, pl.ds(i * rows_of, rows_of), :]

    def whole_meson(which):
        for j in (partner, beyond):
            wait(columns(mesons[which], j), block_sem(which, j))

    def store(out, parts, at):
        for k in range(2):
            for part in range(2):
                out[k, part, at, :] = parts[part][:, k * width:(k + 1) * width].astype(BF16)

    def run(step):
        name, *rest = step.split(".")
        if name == "drain":
            drain(True)
        elif name == "up":
            @pl.when(later > 0)
            def _():
                pl.semaphore_wait(ready, later)

            for i in range(PARTS):
                spread(own(i), meson.at[y], me, i, above(-1), direct & above(-3))
        elif name == "m0":
            i = int(rest[0])
            wait(part_of(m_own, across, i), own_sem(i))
            spread(part_of(m_own, across, i), columns(m_own, across), across, i, None, direct)
        elif name == "m0p":
            send(columns(m_own, across), columns(m_own, across), block_sem(0, across), (tm, partner))
        elif name in ("m1", "m3"):
            which = 1 if name == "m1" else 2
            ref, j = mesons[which], me if rest[0].startswith("me") else across
            if rest[0].endswith("p"):
                if which == 2:
                    wait(columns(ref, j), far_sem(j))
                send(columns(ref, j), columns(ref, j), block_sem(which, j), (tm, partner))
                return
            i = int(rest[1])
            wait(part_of(ref, j, i), near_sem(j, i))
            send(part_of(ref, j, i), part_of(m_far, j, i), far_sem(j), (shifted(-between), me), relays, ("relay", j is me), columns(ref, j))
        elif name in ("adjf1", "adjn1"):
            s, ref, out = (1, p_far, a_far) if name == "adjf1" else (0, p_near, a_near)
            for j in (me, partner):
                wait(columns(ref, j), p_sem.at[s, j])
                adjoint(ref, out, j)
        elif name in ("pf", "pn"):
            s, ref, out = (1, p_far, a_far) if name == "pf" else (0, p_near, a_near)
            wait(columns(ref, across), p_sem.at[s, across])
            send(columns(ref, across), columns(ref, across), p_sem.at[s, across], (tm, partner))
            adjoint(ref, out, across)
        elif name in ("Bf", "Bn"):
            s, ref, adj = (1, p_far, a_far) if name == "Bf" else (0, p_near, a_near)
            if name == first_backward:
                wait(columns(m_own, me), block_sem(0, me))
                whole_meson(0)
            wait(columns(ref, beyond), p_sem.at[s, beyond])
            adjoint(ref, adj, beyond)
            fill_inner(m_own, mine(adj))
            for i in range(CHUNKS):
                at = slice(i * rows_of, (i + 1) * rows_of)
                out = b_out if s else n_out
                store(out, product(ref, at, inner[...]), at)
                for k in range(2):
                    if s:
                        send(piece(out, k, i), piece(b_in, k, i), b_sem.at[k, i], (shifted(between), me), not_direct, "far", out)
                        send(piece(out, k, i), piece(bx_far, k, i), bx_sem.at[1, k, i], (shifted(step_near), me), direct, "cross far", out)
                    else:
                        send(piece(out, k, i), piece(bx_near, k, i), bx_sem.at[0, k, i], (shifted(-step_near), me), direct, "cross near", out)
        elif name == "Fn":
            whole_meson(1)
            fill_inner(m_near, mine(p_near))
            for i in range(CHUNKS):
                at = slice(i * rows_of, (i + 1) * rows_of)
                parts = product(a_near, at, inner[...])
                for part in range(2):
                    f_sum[part, at, :] = parts[part]
        elif name == "Ff":
            whole_meson(2)
            fill_inner(m_far, mine(p_far))
            for i in range(CHUNKS):
                at = slice(i * rows_of, (i + 1) * rows_of)
                parts = product(a_far, at, inner[...])
                store(f_out, (parts[0] + f_sum[0, at, :], parts[1] + f_sum[1, at, :]), at)
            send(f_out.at[1 - y], f_home.at[y], f_sem.at[0], (tm, across))
            local(f_out.at[y], f_home.at[y], f_sem.at[0])
        elif name in ("h1", "h2"):
            k, i = int(rest[0]), int(rest[1])
            at = pl.ds(i * rows_of, rows_of)
            if name == "h1":
                when, out, by = not_direct, s_out, step_near

                @pl.when(when)
                def _():
                    wait(piece(b_in, k, i), b_sem.at[k, i])
                    s_out[k, :, at, :] = (n_out[k, :, at, :].astype(F32) + b_in[k, :, at, :].astype(F32)).astype(BF16)
            else:
                when, out, by = gathers, bx_out, between

                @pl.when(when)
                def _():
                    wait(piece(bx_near, k, i), bx_sem.at[0, k, i])
                    wait(piece(bx_far, k, i), bx_sem.at[1, k, i])
                    bx_out[k, :, at, :] = (bx_near[k, :, at, :].astype(F32) + bx_far[k, :, at, :].astype(F32)).astype(BF16)

            send(piece(out, k, i), piece(b_home, y, i), bh_sem.at[0], (shifted(by), 2 * k + c), when, name, out)

    first_backward = min(("Bf", "Bn"), key=ORDER.index)
    for step in ORDER:
        run(step)

    wait(f_home, f_sem.at[0])
    wait(b_home, bh_sem.at[0])
    drain(False)


def shards(n_tm, n_col, near_prop, far_prop, meson):
    slices, parts, order, width = meson.shape
    whole = pltpu.VMEM((parts, order, order), BF16)
    pair = pltpu.VMEM((2, parts, order, width), BF16)
    home = jax.ShapeDtypeStruct((slices, parts, order, width), BF16)
    dma = pltpu.SemaphoreType.DMA
    forward, backward = pl.pallas_call(
        functools.partial(kernel, n_tm, n_col),
        out_shape=(home, home),
        in_specs=[pl.BlockSpec(memory_space=pl.ANY)] * 3,
        out_specs=[pl.BlockSpec(memory_space=pl.ANY)] * 2,
        scratch_shapes=[
            whole, whole, whole, whole, whole, whole, whole,
            pltpu.VMEM((order, 4 * width), BF16),
            pair, pair, pair, pair, pair, pair, pair,
            pltpu.VMEM((parts, order, 2 * width), F32), pair,
            dma((3 * PARTS + 3 * n_col,)), dma((2, n_col)), dma((2, CHUNKS)), dma((2, 2, CHUNKS)), dma((1,)), dma((1,)), dma((SENDS,)),
            pltpu.SemaphoreType.REGULAR,
        ],
        compiler_params=pltpu.CompilerParams(
            collective_id=0, has_side_effects=True, vmem_limit_bytes=56 * 1024 * 1024
        ),
    )(near_prop, far_prop, meson)
    return forward.astype(F32) + backward.astype(F32)


def solution(mesh):
    spec = P("tm", None, None, "col")
    body = functools.partial(shards, mesh.shape["tm"], mesh.shape["col"])
    return jax.shard_map(body, mesh=mesh, in_specs=(spec, spec, spec), out_specs=spec, check_vma=False)
```

```python
import functools

import jax
import jax.numpy as jnp
from jax import lax
from jax.experimental import pallas as pl
from jax.experimental.pallas import tpu as pltpu
from jax.sharding import PartitionSpec as P

MESH = pl.DeviceIdType.MESH
BF16 = jnp.bfloat16
F32 = jnp.float32
SENDS = 28
EVERY = ()
CHUNKS = 2
PARTS = 4
ORDER = (
    "up", "m0.2", "m0.0", "m1.me.1", "m1.me.2", "m1.me.3", "adjf1", "m0.1",
    "m1.me.0", "m0.3", "pf", "m1.ac.0", "m1.mep", "m1.ac.1", "adjn1", "m1.ac.2",
    "m0p", "m1.ac.3", "Bf", "pn", "m1.acp", "Bn", "Fn", "m3.mep",
    "m3.acp", "h1.0.0", "Ff", "h1.1.0", "drain", "h1.0.1", "h2.0.0", "h1.1.1",
    "h2.1.0", "h2.0.1", "h2.1.1",
)


def kernel(
    n_tm, n_col, near, far, meson, f_home, b_home,
    m_own, m_near, m_far, p_near, p_far, a_near, a_far, inner, b_out, b_in, bx_out, bx_near, bx_far, n_out, s_out, f_sum, f_out,
    m_sem, p_sem, b_sem, bx_sem, f_sem, bh_sem, s_sem, ready,
):
    order = near.shape[2]
    width = near.shape[3]
    half = order // 2
    tile = 2 * width
    tm = lax.axis_index("tm")
    me = lax.axis_index("col")
    y, c = me // 2, me % 2
    step_near, step_far = n_tm // 8, 3 * n_tm // 8
    between = step_far - step_near
    place = tm // step_near
    odd = lax.rem(place, 2)
    partner = 2 * y + 1 - c
    across = 2 * (1 - y) + c
    beyond = 2 * (1 - y) + 1 - c

    def shifted(by):
        return lax.rem(tm + by + n_tm, n_tm)

    def above(by):
        return lax.rem(place + by + 8, 8) > place

    barrier = pltpu.get_barrier_semaphore()
    reach = (1, -1, 2, -2, 3, -3)
    for peer in (partner, across):
        pl.semaphore_signal(barrier, inc=1, device_id=(tm, peer), device_id_type=MESH)
    later = 0
    for by in reach:
        later = later + 2 * above(by).astype(jnp.int32)
        for peer in (me, across):
            @pl.when(above(by))
            def _():
                pl.semaphore_signal(barrier, inc=1, device_id=(shifted(by * step_near), peer), device_id_type=MESH)
    pl.semaphore_wait(barrier, 2 + 2 * len(reach) - later)
    for by in reach:
        for peer in (me, across):
            @pl.when(jnp.logical_not(above(by)))
            def _():
                pl.semaphore_signal(ready, inc=1, device_id=(shifted(by * step_near), peer), device_id_type=MESH)

    groups = {}

    def send(src, dst, recv, device, when=None, group=None, whole=None, waited=None):
        group = len(groups) if group is None else group
        waited = None if waited is EVERY else when if waited is None else waited
        if group not in groups:
            groups[group] = (len(groups), src if whole is None else whole, waited)
        copy = pltpu.make_async_remote_copy(
            src_ref=src, dst_ref=dst, send_sem=s_sem.at[groups[group][0]], recv_sem=recv, device_id=device, device_id_type=MESH
        )
        if when is None:
            copy.start()
        else:
            pl.when(when)(copy.start)

    drained = set()

    def drain(early):
        for group, (n, whole, when) in groups.items():
            if group not in drained and not (early and group in ("h1", "h2")):
                drained.add(group)
                only = pl.when(when) if when is not None else lambda f: f()
                only(pltpu.make_async_copy(whole, whole, s_sem.at[n]).wait)

    def columns(ref, j):
        return ref.at[:, :, pl.ds(pl.multiple_of(j * width, width), width)]

    def wait(ref, sem):
        pltpu.make_async_copy(ref, ref, sem).wait()

    fine = order // PARTS
    rows_of = order // CHUNKS
    mesons = (m_own, m_near, m_far)

    def part_of(ref, j, i):
        return ref.at[:, pl.ds(i * fine, fine), pl.ds(pl.multiple_of(j * width, width), width)]

    direct = (odd == 1) & (c == 1)
    relays = (odd == 1) | (c == 0)
    gathers = (odd == 0) & (c == 1)
    not_direct = jnp.logical_not(direct)

    def spread(src, whole, j, i, when_near, when_far):
        send(src, part_of(m_near, j, i), near_sem(j, i), (shifted(-step_near), me), when_near, ("near", j is me), whole, EVERY)
        send(src, part_of(m_far, j, i), far_sem(j), (shifted(-step_far), me), when_far, ("direct", j is me), whole, direct)

    def own_sem(i):
        return m_sem.at[i]

    def block_sem(which, j):
        return m_sem.at[PARTS + 2 * PARTS + which * n_col + j]

    def near_sem(j, i):
        return m_sem.at[PARTS + (0 if j is me else PARTS) + i]

    def far_sem(j):
        return block_sem(2, j)

    def own(i):
        return meson.at[y, :, pl.ds(i * fine, fine), :]

    def local(src, dst, sem):
        pltpu.make_async_copy(src, dst, sem).start()

    for i in range(PARTS):
        src = meson.at[1 - y, :, pl.ds(i * fine, fine), :]
        send(src, part_of(m_own, me, i), own_sem(i), (tm, across), None, "own", meson.at[1 - y])
    for i in range(PARTS):
        spread(own(i), meson.at[y], me, i, jnp.logical_not(above(-1)), direct & jnp.logical_not(above(-3)))
    send(far.at[1 - y], columns(p_far, me), p_sem.at[1, me], (tm, across))
    send(near.at[1 - y], columns(p_near, me), p_sem.at[0, me], (tm, across))
    for src, ref, sem in ((meson, m_own, block_sem(0, me)), (far, p_far, p_sem.at[1, me]), (near, p_near, p_sem.at[0, me])):
        send(src.at[y], columns(ref, me), sem, (tm, partner))
        local(src.at[y], columns(ref, me), sem)

    rows = lax.broadcasted_iota(jnp.int32, (order, width), 0)

    def adjoint(ref, out, j):
        lanes = lax.broadcasted_iota(jnp.int32, (order, width), 1) + j * width
        sign = jnp.where((rows < half) == (lanes < half), 1.0, -1.0).astype(F32)
        first = pl.multiple_of(j * width, width)
        for part in range(2):
            block = ref[part, :, pl.ds(first, width)].astype(F32) * (sign if part == 0 else -sign)
            out[part, pl.ds(first, width), :] = jnp.transpose(block).astype(BF16)

    def mine(ref):
        picked = []
        for part in range(2):
            for k in range(2):
                picked.append(ref[part, :, pl.ds(pl.multiple_of((2 * k + c) * width, width), width)])
        return jnp.concatenate(picked, axis=1)

    def product(left, at, right):
        first = jnp.dot(left[0, at, :], right, preferred_element_type=F32)
        second = jnp.dot(left[1, at, :], right, preferred_element_type=F32)
        return first[:, :tile] - second[:, tile:], first[:, tile:] + second[:, :tile]

    def fill_inner(left, right):
        for i in range(CHUNKS):
            at = slice(i * rows_of, (i + 1) * rows_of)
            real, imag = product(left, at, right)
            inner[at, :tile] = real.astype(BF16)
            inner[at, tile:] = imag.astype(BF16)

    def piece(ref, k, i):
        return ref.at[k, :, pl.ds(i * rows_of, rows_of), :]

    def whole_meson(which):
        for j in (partner, beyond):
            wait(columns(mesons[which], j), block_sem(which, j))

    def store(out, parts, at):
        for k in range(2):
            for part in range(2):
                out[k, part, at, :] = parts[part][:, k * width:(k + 1) * width].astype(BF16)

    def run(step):
        name, *rest = step.split(".")
        if name == "drain":
            drain(True)
        elif name == "up":
            @pl.when(later > 0)
            def _():
                pl.semaphore_wait(ready, later)

            for i in range(PARTS):
                spread(own(i), meson.at[y], me, i, above(-1), direct & above(-3))
        elif name == "m0":
            i = int(rest[0])
            wait(part_of(m_own, across, i), own_sem(i))
            spread(part_of(m_own, across, i), columns(m_own, across), across, i, None, direct)
        elif name == "m0p":
            send(columns(m_own, across), columns(m_own, across), block_sem(0, across), (tm, partner))
        elif name in ("m1", "m3"):
            which = 1 if name == "m1" else 2
            ref, j = mesons[which], me if rest[0].startswith("me") else across
            if rest[0].endswith("p"):
                if which == 2:
                    wait(columns(ref, j), far_sem(j))
                send(columns(ref, j), columns(ref, j), block_sem(which, j), (tm, partner))
                return
            i = int(rest[1])
            wait(part_of(ref, j, i), near_sem(j, i))
            send(part_of(ref, j, i), part_of(m_far, j, i), far_sem(j), (shifted(-between), me), relays, ("relay", j is me), columns(ref, j))
        elif name in ("adjf1", "adjn1"):
            s, ref, out = (1, p_far, a_far) if name == "adjf1" else (0, p_near, a_near)
            for j in (me, partner):
                wait(columns(ref, j), p_sem.at[s, j])
                adjoint(ref, out, j)
        elif name in ("pf", "pn"):
            s, ref, out = (1, p_far, a_far) if name == "pf" else (0, p_near, a_near)
            wait(columns(ref, across), p_sem.at[s, across])
            send(columns(ref, across), columns(ref, across), p_sem.at[s, across], (tm, partner))
            adjoint(ref, out, across)
        elif name in ("Bf", "Bn"):
            s, ref, adj = (1, p_far, a_far) if name == "Bf" else (0, p_near, a_near)
            if name == first_backward:
                wait(columns(m_own, me), block_sem(0, me))
                whole_meson(0)
            wait(columns(ref, beyond), p_sem.at[s, beyond])
            adjoint(ref, adj, beyond)
            fill_inner(m_own, mine(adj))
            for i in range(CHUNKS):
                at = slice(i * rows_of, (i + 1) * rows_of)
                out = b_out if s else n_out
                store(out, product(ref, at, inner[...]), at)
                for k in range(2):
                    if s:
                        send(piece(out, k, i), piece(b_in, k, i), b_sem.at[k, i], (shifted(between), me), not_direct, "far", out)
                        send(piece(out, k, i), piece(bx_far, k, i), bx_sem.at[1, k, i], (shifted(step_near), me), direct, "cross far", out)
                    else:
                        send(piece(out, k, i), piece(bx_near, k, i), bx_sem.at[0, k, i], (shifted(-step_near), me), direct, "cross near", out)
        elif name == "Fn":
            whole_meson(1)
            fill_inner(m_near, mine(p_near))
            for i in range(CHUNKS):
                at = slice(i * rows_of, (i + 1) * rows_of)
                parts = product(a_near, at, inner[...])
                for part in range(2):
                    f_sum[part, at, :] = parts[part]
        elif name == "Ff":
            whole_meson(2)
            fill_inner(m_far, mine(p_far))
            for i in range(CHUNKS):
                at = slice(i * rows_of, (i + 1) * rows_of)
                parts = product(a_far, at, inner[...])
                store(f_out, (parts[0] + f_sum[0, at, :], parts[1] + f_sum[1, at, :]), at)
            send(f_out.at[1 - y], f_home.at[y], f_sem.at[0], (tm, across))
            local(f_out.at[y], f_home.at[y], f_sem.at[0])
        elif name in ("h1", "h2"):
            k, i = int(rest[0]), int(rest[1])
            at = pl.ds(i * rows_of, rows_of)
            if name == "h1":
                when, out, by = not_direct, s_out, step_near

                @pl.when(when)
                def _():
                    wait(piece(b_in, k, i), b_sem.at[k, i])
                    s_out[k, :, at, :] = (n_out[k, :, at, :].astype(F32) + b_in[k, :, at, :].astype(F32)).astype(BF16)
            else:
                when, out, by = gathers, bx_out, between

                @pl.when(when)
                def _():
                    wait(piece(bx_near, k, i), bx_sem.at[0, k, i])
                    wait(piece(bx_far, k, i), bx_sem.at[1, k, i])
                    bx_out[k, :, at, :] = (bx_near[k, :, at, :].astype(F32) + bx_far[k, :, at, :].astype(F32)).astype(BF16)

            send(piece(out, k, i), piece(b_home, y, i), bh_sem.at[0], (shifted(by), 2 * k + c), when, name, out)

    first_backward = min(("Bf", "Bn"), key=ORDER.index)
    for step in ORDER:
        run(step)

    wait(f_home, f_sem.at[0])
    wait(b_home, bh_sem.at[0])
    drain(False)


def shards(n_tm, n_col, near_prop, far_prop, meson):
    slices, parts, order, width = meson.shape
    whole = pltpu.VMEM((parts, order, order), BF16)
    pair = pltpu.VMEM((2, parts, order, width), BF16)
    home = jax.ShapeDtypeStruct((slices, parts, order, width), BF16)
    dma = pltpu.SemaphoreType.DMA
    forward, backward = pl.pallas_call(
        functools.partial(kernel, n_tm, n_col),
        out_shape=(home, home),
        in_specs=[pl.BlockSpec(memory_space=pl.ANY)] * 3,
        out_specs=[pl.BlockSpec(memory_space=pl.ANY)] * 2,
        scratch_shapes=[
            whole, whole, whole, whole, whole, whole, whole,
            pltpu.VMEM((order, 4 * width), BF16),
            pair, pair, pair, pair, pair, pair, pair,
            pltpu.VMEM((parts, order, 2 * width), F32), pair,
            dma((3 * PARTS + 3 * n_col,)), dma((2, n_col)), dma((2, CHUNKS)), dma((2, 2, CHUNKS)), dma((1,)), dma((1,)), dma((SENDS,)),
            pltpu.SemaphoreType.REGULAR,
        ],
        compiler_params=pltpu.CompilerParams(
            collective_id=0, has_side_effects=True, vmem_limit_bytes=105 * 512 * 1024
        ),
    )(near_prop, far_prop, meson)
    return forward.astype(F32) + backward.astype(F32)


def solution(mesh):
    spec = P("tm", None, None, "col")
    body = functools.partial(shards, mesh.shape["tm"], mesh.shape["col"])
    return jax.shard_map(body, mesh=mesh, in_specs=(spec, spec, spec), out_specs=spec, check_vma=False)
```

```python
import functools

import jax
import jax.numpy as jnp
from jax import lax
from jax.experimental import pallas as pl
from jax.experimental.pallas import tpu as pltpu
from jax.sharding import PartitionSpec as P

MESH = pl.DeviceIdType.MESH
BF16 = jnp.bfloat16
F32 = jnp.float32
SENDS = 28
EVERY = ()
CHUNKS = 2
PARTS = 4
ORDER = (
    "up", "m0.2", "m0.0", "m1.me.1", "m1.me.2", "m1.me.3", "adjf1", "adjn1",
    "m0.1", "m1.me.0", "m0.3", "pf", "m0p", "m1.ac.0", "m1.mep", "m1.ac.1",
    "m1.ac.2", "m1.ac.3", "Bf", "pn", "m1.acp", "Bn", "Fn", "m3.mep",
    "m3.acp", "h1.0.0", "e1.1.0", "Ff", "l1.1.0", "drain", "h1.0.1", "h2.0.0",
    "h1.1.1", "h2.1.0", "h2.0.1", "h2.1.1",
)


def kernel(
    n_tm, n_col, near, far, meson, f_home, b_home,
    m_own, m_near, m_far, p_near, p_far, a_near, a_far, inner, b_out, b_in, bx_out, bx_near, bx_far, n_out, s_out, f_sum, f_out,
    m_sem, p_sem, b_sem, bx_sem, f_sem, bh_sem, s_sem, ready,
):
    order = near.shape[2]
    width = near.shape[3]
    half = order // 2
    tile = 2 * width
    tm = lax.axis_index("tm")
    me = lax.axis_index("col")
    y, c = me // 2, me % 2
    step_near, step_far = n_tm // 8, 3 * n_tm // 8
    between = step_far - step_near
    place = tm // step_near
    odd = lax.rem(place, 2)
    partner = 2 * y + 1 - c
    across = 2 * (1 - y) + c
    beyond = 2 * (1 - y) + 1 - c

    def shifted(by):
        return lax.rem(tm + by + n_tm, n_tm)

    def above(by):
        return lax.rem(place + by + 8, 8) > place

    barrier = pltpu.get_barrier_semaphore()
    reach = (1, -1, 2, -2, 3, -3)
    for peer in (partner, across):
        pl.semaphore_signal(barrier, inc=1, device_id=(tm, peer), device_id_type=MESH)
    later = 0
    for by in reach:
        later = later + (2 if abs(by) < 3 else 1) * above(by).astype(jnp.int32)
        for peer in ((me, across) if abs(by) < 3 else (me,)):
            @pl.when(above(by))
            def _():
                pl.semaphore_signal(barrier, inc=1, device_id=(shifted(by * step_near), peer), device_id_type=MESH)
    pl.semaphore_wait(barrier, 2 * len(reach) - later)
    for by in reach:
        for peer in ((me, across) if abs(by) < 3 else (me,)):
            @pl.when(jnp.logical_not(above(by)))
            def _():
                pl.semaphore_signal(ready, inc=1, device_id=(shifted(by * step_near), peer), device_id_type=MESH)

    groups = {}

    def send(src, dst, recv, device, when=None, group=None, whole=None, waited=None):
        group = len(groups) if group is None else group
        waited = None if waited is EVERY else when if waited is None else waited
        if group not in groups:
            groups[group] = (len(groups), src if whole is None else whole, waited)
        copy = pltpu.make_async_remote_copy(
            src_ref=src, dst_ref=dst, send_sem=s_sem.at[groups[group][0]], recv_sem=recv, device_id=device, device_id_type=MESH
        )
        if when is None:
            copy.start()
        else:
            pl.when(when)(copy.start)

    drained = set()

    def drain(early):
        for group, (n, whole, when) in groups.items():
            if group not in drained and not (early and group in ("h1", "h2")):
                drained.add(group)
                only = pl.when(when) if when is not None else lambda f: f()
                only(pltpu.make_async_copy(whole, whole, s_sem.at[n]).wait)

    def columns(ref, j):
        return ref.at[:, :, pl.ds(pl.multiple_of(j * width, width), width)]

    def wait(ref, sem):
        pltpu.make_async_copy(ref, ref, sem).wait()

    fine = order // PARTS
    rows_of = order // CHUNKS
    mesons = (m_own, m_near, m_far)

    def part_of(ref, j, i):
        return ref.at[:, pl.ds(i * fine, fine), pl.ds(pl.multiple_of(j * width, width), width)]

    direct = (odd == 1) & (c == 1)
    relays = (odd == 1) | (c == 0)
    gathers = (odd == 0) & (c == 1)
    not_direct = jnp.logical_not(direct)

    def spread(src, whole, j, i, when_near, when_far):
        send(src, part_of(m_near, j, i), near_sem(j, i), (shifted(-step_near), me), when_near, ("near", j is me), whole, EVERY)
        send(src, part_of(m_far, j, i), far_sem(j), (shifted(-step_far), me), when_far, ("direct", j is me), whole, direct)

    def own_sem(i):
        return m_sem.at[i]

    def block_sem(which, j):
        return m_sem.at[PARTS + 2 * PARTS + which * n_col + j]

    def near_sem(j, i):
        return m_sem.at[PARTS + (0 if j is me else PARTS) + i]

    def far_sem(j):
        return block_sem(2, j)

    def own(i):
        return meson.at[y, :, pl.ds(i * fine, fine), :]

    def local(src, dst, sem):
        pltpu.make_async_copy(src, dst, sem).start()

    for i in range(PARTS):
        src = meson.at[1 - y, :, pl.ds(i * fine, fine), :]
        send(src, part_of(m_own, me, i), own_sem(i), (tm, across), None, "own", meson.at[1 - y])
    for i in range(PARTS):
        spread(own(i), meson.at[y], me, i, jnp.logical_not(above(-1)), direct & jnp.logical_not(above(-3)))
    send(far.at[1 - y], columns(p_far, me), p_sem.at[1, me], (tm, across))
    send(near.at[1 - y], columns(p_near, me), p_sem.at[0, me], (tm, across))
    for src, ref, sem in ((meson, m_own, block_sem(0, me)), (far, p_far, p_sem.at[1, me]), (near, p_near, p_sem.at[0, me])):
        send(src.at[y], columns(ref, me), sem, (tm, partner))
        local(src.at[y], columns(ref, me), sem)

    rows = lax.broadcasted_iota(jnp.int32, (order, width), 0)

    def adjoint(ref, out, j):
        lanes = lax.broadcasted_iota(jnp.int32, (order, width), 1) + j * width
        sign = jnp.where((rows < half) == (lanes < half), 1.0, -1.0).astype(F32)
        first = pl.multiple_of(j * width, width)
        for part in range(2):
            block = ref[part, :, pl.ds(first, width)].astype(F32) * (sign if part == 0 else -sign)
            out[part, pl.ds(first, width), :] = jnp.transpose(block).astype(BF16)

    def mine(ref):
        picked = []
        for part in range(2):
            for k in range(2):
                picked.append(ref[part, :, pl.ds(pl.multiple_of((2 * k + c) * width, width), width)])
        return jnp.concatenate(picked, axis=1)

    def product(left, at, right):
        first = jnp.dot(left[0, at, :], right, preferred_element_type=F32)
        second = jnp.dot(left[1, at, :], right, preferred_element_type=F32)
        return first[:, :tile] - second[:, tile:], first[:, tile:] + second[:, :tile]

    def fill_inner(left, right):
        for i in range(CHUNKS):
            at = slice(i * rows_of, (i + 1) * rows_of)
            real, imag = product(left, at, right)
            inner[at, :tile] = real.astype(BF16)
            inner[at, tile:] = imag.astype(BF16)

    def piece(ref, k, i):
        return ref.at[k, :, pl.ds(i * rows_of, rows_of), :]

    def whole_meson(which):
        for j in (partner, beyond):
            wait(columns(mesons[which], j), block_sem(which, j))

    def store(out, parts, at):
        for k in range(2):
            for part in range(2):
                out[k, part, at, :] = parts[part][:, k * width:(k + 1) * width].astype(BF16)

    def run(step):
        name, *rest = step.split(".")
        if name == "drain":
            drain(True)
        elif name == "up":
            @pl.when(later > 0)
            def _():
                pl.semaphore_wait(ready, later)

            for i in range(PARTS):
                spread(own(i), meson.at[y], me, i, above(-1), direct & above(-3))
        elif name == "m0":
            i = int(rest[0])
            wait(part_of(m_own, across, i), own_sem(i))
            spread(part_of(m_own, across, i), columns(m_own, across), across, i, None, direct)
        elif name == "m0p":
            send(columns(m_own, across), columns(m_own, across), block_sem(0, across), (tm, partner))
        elif name in ("m1", "m3"):
            which = 1 if name == "m1" else 2
            ref, j = mesons[which], me if rest[0].startswith("me") else across
            if rest[0].endswith("p"):
                if which == 2:
                    wait(columns(ref, j), far_sem(j))
                send(columns(ref, j), columns(ref, j), block_sem(which, j), (tm, partner))
                return
            i = int(rest[1])
            wait(part_of(ref, j, i), near_sem(j, i))
            send(part_of(ref, j, i), part_of(m_far, j, i), far_sem(j), (shifted(-between), me), relays, ("relay", j is me), columns(ref, j))
        elif name in ("adjf1", "adjn1"):
            s, ref, out = (1, p_far, a_far) if name == "adjf1" else (0, p_near, a_near)
            for j in (me, partner):
                wait(columns(ref, j), p_sem.at[s, j])
                adjoint(ref, out, j)
        elif name in ("pf", "pn"):
            s, ref, out = (1, p_far, a_far) if name == "pf" else (0, p_near, a_near)
            wait(columns(ref, across), p_sem.at[s, across])
            send(columns(ref, across), columns(ref, across), p_sem.at[s, across], (tm, partner))
            adjoint(ref, out, across)
        elif name in ("Bf", "Bn"):
            s, ref, adj = (1, p_far, a_far) if name == "Bf" else (0, p_near, a_near)
            if name == first_backward:
                wait(columns(m_own, me), block_sem(0, me))
                whole_meson(0)
            wait(columns(ref, beyond), p_sem.at[s, beyond])
            adjoint(ref, adj, beyond)
            fill_inner(m_own, mine(adj))
            for i in range(CHUNKS):
                at = slice(i * rows_of, (i + 1) * rows_of)
                out = b_out if s else n_out
                store(out, product(ref, at, inner[...]), at)
                for k in range(2):
                    if s:
                        send(piece(out, k, i), piece(b_in, k, i), b_sem.at[k, i], (shifted(between), me), not_direct, "far", out)
                        send(piece(out, k, i), piece(bx_far, k, i), bx_sem.at[1, k, i], (shifted(step_near), me), direct, "cross far", out)
                    else:
                        send(piece(out, k, i), piece(bx_near, k, i), bx_sem.at[0, k, i], (shifted(-step_near), me), direct, "cross near", out)
        elif name == "Fn":
            whole_meson(1)
            fill_inner(m_near, mine(p_near))
            for i in range(CHUNKS):
                at = slice(i * rows_of, (i + 1) * rows_of)
                parts = product(a_near, at, inner[...])
                for part in range(2):
                    f_sum[part, at, :] = parts[part]
        elif name == "Ff":
            whole_meson(2)
            fill_inner(m_far, mine(p_far))
            for i in range(CHUNKS):
                at = slice(i * rows_of, (i + 1) * rows_of)
                parts = product(a_far, at, inner[...])
                store(f_out, (parts[0] + f_sum[0, at, :], parts[1] + f_sum[1, at, :]), at)
            send(f_out.at[1 - y], f_home.at[y], f_sem.at[0], (tm, across))
            local(f_out.at[y], f_home.at[y], f_sem.at[0])
        elif name in ("h1", "h2", "e1", "l1"):
            k, i = int(rest[0]), int(rest[1])
            at = pl.ds(i * rows_of, rows_of)
            if name != "h2":
                when, out, by = not_direct, s_out, step_near
                if name != "h1":
                    when = when & (place >= 4 if name == "e1" else place < 4)

                @pl.when(when)
                def _():
                    wait(piece(b_in, k, i), b_sem.at[k, i])
                    s_out[k, :, at, :] = (n_out[k, :, at, :].astype(F32) + b_in[k, :, at, :].astype(F32)).astype(BF16)
            else:
                when, out, by = gathers, bx_out, between

                @pl.when(when)
                def _():
                    wait(piece(bx_near, k, i), bx_sem.at[0, k, i])
                    wait(piece(bx_far, k, i), bx_sem.at[1, k, i])
                    bx_out[k, :, at, :] = (bx_near[k, :, at, :].astype(F32) + bx_far[k, :, at, :].astype(F32)).astype(BF16)

            send(piece(out, k, i), piece(b_home, y, i), bh_sem.at[0], (shifted(by), 2 * k + c), when, "h2" if name == "h2" else "h1", out, gathers if name == "h2" else not_direct)

    first_backward = min(("Bf", "Bn"), key=ORDER.index)
    for step in ORDER:
        run(step)

    wait(f_home, f_sem.at[0])
    wait(b_home, bh_sem.at[0])
    drain(False)


def shards(n_tm, n_col, near_prop, far_prop, meson):
    slices, parts, order, width = meson.shape
    whole = pltpu.VMEM((parts, order, order), BF16)
    pair = pltpu.VMEM((2, parts, order, width), BF16)
    home = jax.ShapeDtypeStruct((slices, parts, order, width), BF16)
    dma = pltpu.SemaphoreType.DMA
    forward, backward = pl.pallas_call(
        functools.partial(kernel, n_tm, n_col),
        out_shape=(home, home),
        in_specs=[pl.BlockSpec(memory_space=pl.ANY)] * 3,
        out_specs=[pl.BlockSpec(memory_space=pl.ANY)] * 2,
        scratch_shapes=[
            whole, whole, whole, whole, whole, whole, whole,
            pltpu.VMEM((order, 4 * width), BF16),
            pair, pair, pair, pair, pair, pair, pair,
            pltpu.VMEM((parts, order, 2 * width), F32), pair,
            dma((3 * PARTS + 3 * n_col,)), dma((2, n_col)), dma((2, CHUNKS)), dma((2, 2, CHUNKS)), dma((1,)), dma((1,)), dma((SENDS,)),
            pltpu.SemaphoreType.REGULAR,
        ],
        compiler_params=pltpu.CompilerParams(
            collective_id=0, has_side_effects=True, vmem_limit_bytes=105 * 512 * 1024
        ),
    )(near_prop, far_prop, meson)
    return forward.astype(F32) + backward.astype(F32)


def solution(mesh):
    spec = P("tm", None, None, "col")
    body = functools.partial(shards, mesh.shape["tm"], mesh.shape["col"])
    return jax.shard_map(body, mesh=mesh, in_specs=(spec, spec, spec), out_specs=spec, check_vma=False)
```

```python
import functools

import jax
import jax.numpy as jnp
from jax import lax
from jax.experimental import pallas as pl
from jax.experimental.pallas import tpu as pltpu
from jax.sharding import PartitionSpec as P

MESH = pl.DeviceIdType.MESH
BF16 = jnp.bfloat16
F32 = jnp.float32
SENDS = 28
EVERY = ()
CHUNKS = 2
PARTS = 4
ORDER = (
    "up", "m0.2", "m0.0", "m1.me.1", "m1.me.2", "m1.me.3", "adjf1", "adjn1",
    "m0.1", "m1.me.0", "m0.3", "pf", "m0p", "m1.ac.0", "m1.mep", "m1.ac.1",
    "m1.ac.2", "m1.ac.3", "Bf", "pn", "m1.acp", "Bn", "Fn", "m3.mep",
    "m3.acp", "h1.0.0", "e1.1.0", "Ff", "l1.1.0", "h1.0.1", "drain", "h2.0.0",
    "h1.1.1", "h2.1.0", "h2.0.1", "h2.1.1",
)


def kernel(
    n_tm, n_col, near, far, meson, f_home, b_home,
    m_own, m_near, m_far, p_near, p_far, a_near, a_far, inner, b_out, b_in, bx_out, bx_near, bx_far, n_out, s_out, f_sum, f_out,
    m_sem, p_sem, b_sem, bx_sem, f_sem, bh_sem, s_sem, ready,
):
    order = near.shape[2]
    width = near.shape[3]
    half = order // 2
    tile = 2 * width
    tm = lax.axis_index("tm")
    me = lax.axis_index("col")
    y, c = me // 2, me % 2
    step_near, step_far = n_tm // 8, 3 * n_tm // 8
    between = step_far - step_near
    place = tm // step_near
    odd = lax.rem(place, 2)
    partner = 2 * y + 1 - c
    across = 2 * (1 - y) + c
    beyond = 2 * (1 - y) + 1 - c

    def shifted(by):
        return lax.rem(tm + by + n_tm, n_tm)

    def above(by):
        return lax.rem(place + by + 8, 8) > place

    barrier = pltpu.get_barrier_semaphore()
    reach = (1, -1, 2, -2, 3, -3)
    for peer in (partner, across):
        pl.semaphore_signal(barrier, inc=1, device_id=(tm, peer), device_id_type=MESH)
    later = 0
    for by in reach:
        later = later + (2 if abs(by) < 3 else 1) * above(by).astype(jnp.int32)
        for peer in ((me, across) if abs(by) < 3 else (me,)):
            @pl.when(above(by))
            def _():
                pl.semaphore_signal(barrier, inc=1, device_id=(shifted(by * step_near), peer), device_id_type=MESH)
    pl.semaphore_wait(barrier, 2 * len(reach) - later)
    for by in reach:
        for peer in ((me, across) if abs(by) < 3 else (me,)):
            @pl.when(jnp.logical_not(above(by)))
            def _():
                pl.semaphore_signal(ready, inc=1, device_id=(shifted(by * step_near), peer), device_id_type=MESH)

    groups = {}

    def send(src, dst, recv, device, when=None, group=None, whole=None, waited=None):
        group = len(groups) if group is None else group
        waited = None if waited is EVERY else when if waited is None else waited
        if group not in groups:
            groups[group] = (len(groups), src if whole is None else whole, waited)
        copy = pltpu.make_async_remote_copy(
            src_ref=src, dst_ref=dst, send_sem=s_sem.at[groups[group][0]], recv_sem=recv, device_id=device, device_id_type=MESH
        )
        if when is None:
            copy.start()
        else:
            pl.when(when)(copy.start)

    drained = set()

    def drain(early):
        for group, (n, whole, when) in groups.items():
            if group not in drained and not (early and group in ("h1", "h2")):
                drained.add(group)
                only = pl.when(when) if when is not None else lambda f: f()
                only(pltpu.make_async_copy(whole, whole, s_sem.at[n]).wait)

    def columns(ref, j):
        return ref.at[:, :, pl.ds(pl.multiple_of(j * width, width), width)]

    def wait(ref, sem):
        pltpu.make_async_copy(ref, ref, sem).wait()

    fine = order // PARTS
    rows_of = order // CHUNKS
    mesons = (m_own, m_near, m_far)

    def part_of(ref, j, i):
        return ref.at[:, pl.ds(i * fine, fine), pl.ds(pl.multiple_of(j * width, width), width)]

    direct = (odd == 1) & (c == 1)
    relays = (odd == 1) | (c == 0)
    gathers = (odd == 0) & (c == 1)
    not_direct = jnp.logical_not(direct)

    def spread(src, whole, j, i, when_near, when_far):
        send(src, part_of(m_near, j, i), near_sem(j, i), (shifted(-step_near), me), when_near, ("near", j is me), whole, EVERY)
        send(src, part_of(m_far, j, i), far_sem(j), (shifted(-step_far), me), when_far, ("direct", j is me), whole, direct)

    def own_sem(i):
        return m_sem.at[i]

    def block_sem(which, j):
        return m_sem.at[PARTS + 2 * PARTS + which * n_col + j]

    def near_sem(j, i):
        return m_sem.at[PARTS + (0 if j is me else PARTS) + i]

    def far_sem(j):
        return block_sem(2, j)

    def own(i):
        return meson.at[y, :, pl.ds(i * fine, fine), :]

    def local(src, dst, sem):
        pltpu.make_async_copy(src, dst, sem).start()

    for i in range(PARTS):
        src = meson.at[1 - y, :, pl.ds(i * fine, fine), :]
        send(src, part_of(m_own, me, i), own_sem(i), (tm, across), None, "own", meson.at[1 - y])
    for i in range(PARTS):
        spread(own(i), meson.at[y], me, i, jnp.logical_not(above(-1)), direct & jnp.logical_not(above(-3)))
    send(far.at[1 - y], columns(p_far, me), p_sem.at[1, me], (tm, across))
    send(near.at[1 - y], columns(p_near, me), p_sem.at[0, me], (tm, across))
    for src, ref, sem in ((meson, m_own, block_sem(0, me)), (far, p_far, p_sem.at[1, me]), (near, p_near, p_sem.at[0, me])):
        send(src.at[y], columns(ref, me), sem, (tm, partner))
        local(src.at[y], columns(ref, me), sem)

    rows = lax.broadcasted_iota(jnp.int32, (order, width), 0)

    def adjoint(ref, out, j):
        lanes = lax.broadcasted_iota(jnp.int32, (order, width), 1) + j * width
        sign = jnp.where((rows < half) == (lanes < half), 1.0, -1.0).astype(F32)
        first = pl.multiple_of(j * width, width)
        for part in range(2):
            block = ref[part, :, pl.ds(first, width)].astype(F32) * (sign if part == 0 else -sign)
            out[part, pl.ds(first, width), :] = jnp.transpose(block).astype(BF16)

    def mine(ref):
        picked = []
        for part in range(2):
            for k in range(2):
                picked.append(ref[part, :, pl.ds(pl.multiple_of((2 * k + c) * width, width), width)])
        return jnp.concatenate(picked, axis=1)

    def product(left, at, right):
        first = jnp.dot(left[0, at, :], right, preferred_element_type=F32)
        second = jnp.dot(left[1, at, :], right, preferred_element_type=F32)
        return first[:, :tile] - second[:, tile:], first[:, tile:] + second[:, :tile]

    def fill_inner(left, right):
        for i in range(CHUNKS):
            at = slice(i * rows_of, (i + 1) * rows_of)
            real, imag = product(left, at, right)
            inner[at, :tile] = real.astype(BF16)
            inner[at, tile:] = imag.astype(BF16)

    def piece(ref, k, i):
        return ref.at[k, :, pl.ds(i * rows_of, rows_of), :]

    def whole_meson(which):
        for j in (partner, beyond):
            wait(columns(mesons[which], j), block_sem(which, j))

    def store(out, parts, at):
        for k in range(2):
            for part in range(2):
                out[k, part, at, :] = parts[part][:, k * width:(k + 1) * width].astype(BF16)

    def run(step):
        name, *rest = step.split(".")
        if name == "drain":
            drain(True)
        elif name == "up":
            @pl.when(later > 0)
            def _():
                pl.semaphore_wait(ready, later)

            for i in range(PARTS):
                spread(own(i), meson.at[y], me, i, above(-1), direct & above(-3))
        elif name == "m0":
            i = int(rest[0])
            wait(part_of(m_own, across, i), own_sem(i))
            spread(part_of(m_own, across, i), columns(m_own, across), across, i, None, direct)
        elif name == "m0p":
            send(columns(m_own, across), columns(m_own, across), block_sem(0, across), (tm, partner))
        elif name in ("m1", "m3"):
            which = 1 if name == "m1" else 2
            ref, j = mesons[which], me if rest[0].startswith("me") else across
            if rest[0].endswith("p"):
                if which == 2:
                    wait(columns(ref, j), far_sem(j))
                send(columns(ref, j), columns(ref, j), block_sem(which, j), (tm, partner))
                return
            i = int(rest[1])
            wait(part_of(ref, j, i), near_sem(j, i))
            send(part_of(ref, j, i), part_of(m_far, j, i), far_sem(j), (shifted(-between), me), relays, ("relay", j is me), columns(ref, j))
        elif name in ("adjf1", "adjn1"):
            s, ref, out = (1, p_far, a_far) if name == "adjf1" else (0, p_near, a_near)
            for j in (me, partner):
                wait(columns(ref, j), p_sem.at[s, j])
                adjoint(ref, out, j)
        elif name in ("pf", "pn"):
            s, ref, out = (1, p_far, a_far) if name == "pf" else (0, p_near, a_near)
            wait(columns(ref, across), p_sem.at[s, across])
            send(columns(ref, across), columns(ref, across), p_sem.at[s, across], (tm, partner))
            adjoint(ref, out, across)
        elif name in ("Bf", "Bn"):
            s, ref, adj = (1, p_far, a_far) if name == "Bf" else (0, p_near, a_near)
            if name == first_backward:
                wait(columns(m_own, me), block_sem(0, me))
                whole_meson(0)
            wait(columns(ref, beyond), p_sem.at[s, beyond])
            adjoint(ref, adj, beyond)
            fill_inner(m_own, mine(adj))
            for i in range(CHUNKS):
                at = slice(i * rows_of, (i + 1) * rows_of)
                out = b_out if s else n_out
                store(out, product(ref, at, inner[...]), at)
                for k in range(2):
                    if s:
                        send(piece(out, k, i), piece(b_in, k, i), b_sem.at[k, i], (shifted(between), me), not_direct, "far", out)
                        send(piece(out, k, i), piece(bx_far, k, i), bx_sem.at[1, k, i], (shifted(step_near), me), direct, "cross far", out)
                    else:
                        send(piece(out, k, i), piece(bx_near, k, i), bx_sem.at[0, k, i], (shifted(-step_near), me), direct, "cross near", out)
        elif name == "Fn":
            whole_meson(1)
            fill_inner(m_near, mine(p_near))
            for i in range(CHUNKS):
                at = slice(i * rows_of, (i + 1) * rows_of)
                parts = product(a_near, at, inner[...])
                for part in range(2):
                    f_sum[part, at, :] = parts[part]
        elif name == "Ff":
            whole_meson(2)
            fill_inner(m_far, mine(p_far))
            for i in range(CHUNKS):
                at = slice(i * rows_of, (i + 1) * rows_of)
                parts = product(a_far, at, inner[...])
                store(f_out, (parts[0] + f_sum[0, at, :], parts[1] + f_sum[1, at, :]), at)
            send(f_out.at[1 - y], f_home.at[y], f_sem.at[0], (tm, across))
            local(f_out.at[y], f_home.at[y], f_sem.at[0])
        elif name in ("h1", "h2", "e1", "l1"):
            k, i = int(rest[0]), int(rest[1])
            at = pl.ds(i * rows_of, rows_of)
            if name != "h2":
                when, out, by = not_direct, s_out, step_near
                if name != "h1":
                    when = when & (place >= 4 if name == "e1" else place < 4)

                @pl.when(when)
                def _():
                    wait(piece(b_in, k, i), b_sem.at[k, i])
                    s_out[k, :, at, :] = (n_out[k, :, at, :].astype(F32) + b_in[k, :, at, :].astype(F32)).astype(BF16)
            else:
                when, out, by = gathers, bx_out, between

                @pl.when(when)
                def _():
                    wait(piece(bx_near, k, i), bx_sem.at[0, k, i])
                    wait(piece(bx_far, k, i), bx_sem.at[1, k, i])
                    bx_out[k, :, at, :] = (bx_near[k, :, at, :].astype(F32) + bx_far[k, :, at, :].astype(F32)).astype(BF16)

            send(piece(out, k, i), piece(b_home, y, i), bh_sem.at[0], (shifted(by), 2 * k + c), when, "h2" if name == "h2" else "h1", out, gathers if name == "h2" else not_direct)

    first_backward = min(("Bf", "Bn"), key=ORDER.index)
    for step in ORDER:
        run(step)

    wait(f_home, f_sem.at[0])
    wait(b_home, bh_sem.at[0])
    drain(False)


def shards(n_tm, n_col, near_prop, far_prop, meson):
    slices, parts, order, width = meson.shape
    whole = pltpu.VMEM((parts, order, order), BF16)
    pair = pltpu.VMEM((2, parts, order, width), BF16)
    home = jax.ShapeDtypeStruct((slices, parts, order, width), BF16)
    dma = pltpu.SemaphoreType.DMA
    forward, backward = pl.pallas_call(
        functools.partial(kernel, n_tm, n_col),
        out_shape=(home, home),
        in_specs=[pl.BlockSpec(memory_space=pl.ANY)] * 3,
        out_specs=[pl.BlockSpec(memory_space=pl.ANY)] * 2,
        scratch_shapes=[
            whole, whole, whole, whole, whole, whole, whole,
            pltpu.VMEM((order, 4 * width), BF16),
            pair, pair, pair, pair, pair, pair, pair,
            pltpu.VMEM((parts, order, 2 * width), F32), pair,
            dma((3 * PARTS + 3 * n_col,)), dma((2, n_col)), dma((2, CHUNKS)), dma((2, 2, CHUNKS)), dma((1,)), dma((1,)), dma((SENDS,)),
            pltpu.SemaphoreType.REGULAR,
        ],
        compiler_params=pltpu.CompilerParams(
            collective_id=0, has_side_effects=True, vmem_limit_bytes=105 * 512 * 1024
        ),
    )(near_prop, far_prop, meson)
    return forward.astype(F32) + backward.astype(F32)


def solution(mesh):
    spec = P("tm", None, None, "col")
    body = functools.partial(shards, mesh.shape["tm"], mesh.shape["col"])
    return jax.shard_map(body, mesh=mesh, in_specs=(spec, spec, spec), out_specs=spec, check_vma=False)
```

```python
import functools

import jax
import jax.numpy as jnp
from jax import lax
from jax.experimental import pallas as pl
from jax.experimental.pallas import tpu as pltpu
from jax.sharding import PartitionSpec as P

MESH = pl.DeviceIdType.MESH
BF16 = jnp.bfloat16
F32 = jnp.float32
SENDS = 25
EVERY = ()
CHUNKS = 2
PARTS = 4
ORDER = (
    "up", "m0.2", "m0.0", "m1.me.1", "m1.me.2", "m1.me.3", "adjf1", "adjn1",
    "m0.1", "m1.me.0", "m0.3", "pf", "m0p", "m1.ac.0", "m1.mep", "m1.ac.1",
    "m1.ac.2", "m1.ac.3", "Bf", "pn", "m1.acp", "Bn", "Fn", "m3.mep",
    "m3.acp", "h1.0.0", "e1.1.0", "Ff", "l1.1.0", "drain", "h1.0.1", "h2.0.0",
    "h1.1.1", "h2.1.0", "h2.0.1", "h2.1.1",
)


def kernel(
    n_tm, n_col, near, far, meson, f_home, b_home,
    m_own, m_near, m_far, p_near, p_far, a_near, a_far, inner, b_out, b_in, bx_out, bx_near, bx_far, n_out, s_out, f_sum, f_out,
    m_sem, p_sem, b_sem, bx_sem, f_sem, bh_sem, s_sem, ready,
):
    order = near.shape[2]
    width = near.shape[3]
    half = order // 2
    tile = 2 * width
    tm = lax.axis_index("tm")
    me = lax.axis_index("col")
    y, c = me // 2, me % 2
    step_near, step_far = n_tm // 8, 3 * n_tm // 8
    between = step_far - step_near
    place = tm // step_near
    odd = lax.rem(place, 2)
    partner = 2 * y + 1 - c
    across = 2 * (1 - y) + c
    beyond = 2 * (1 - y) + 1 - c

    def shifted(by):
        return lax.rem(tm + by + n_tm, n_tm)

    def above(by):
        return lax.rem(place + by + 8, 8) > place

    barrier = pltpu.get_barrier_semaphore()
    reach = (1, -1, 2, -2, 3, -3)
    for peer in (partner, across):
        pl.semaphore_signal(barrier, inc=1, device_id=(tm, peer), device_id_type=MESH)
    later = 0
    for by in reach:
        later = later + (2 if abs(by) < 3 else 1) * above(by).astype(jnp.int32)
        for peer in ((me, across) if abs(by) < 3 else (me,)):
            @pl.when(above(by))
            def _():
                pl.semaphore_signal(barrier, inc=1, device_id=(shifted(by * step_near), peer), device_id_type=MESH)
    pl.semaphore_wait(barrier, 2 * len(reach) - later)
    for by in reach:
        for peer in ((me, across) if abs(by) < 3 else (me,)):
            @pl.when(jnp.logical_not(above(by)))
            def _():
                pl.semaphore_signal(ready, inc=1, device_id=(shifted(by * step_near), peer), device_id_type=MESH)

    groups = {}

    def send(src, dst, recv, device, when=None, group=None, whole=None, waited=None):
        group = len(groups) if group is None else group
        waited = None if waited is EVERY else when if waited is None else waited
        if group not in groups:
            groups[group] = (len(groups), src if whole is None else whole, waited)
        copy = pltpu.make_async_remote_copy(
            src_ref=src, dst_ref=dst, send_sem=s_sem.at[groups[group][0]], recv_sem=recv, device_id=device, device_id_type=MESH
        )
        if when is None:
            copy.start()
        else:
            pl.when(when)(copy.start)

    drained = set()

    def drain(early):
        for group, (n, whole, when) in groups.items():
            if group not in drained and not (early and group in ("h1", "h2")):
                drained.add(group)
                only = pl.when(when) if when is not None else lambda f: f()
                only(pltpu.make_async_copy(whole, whole, s_sem.at[n]).wait)

    def columns(ref, j):
        return ref.at[:, :, pl.ds(pl.multiple_of(j * width, width), width)]

    def wait(ref, sem):
        pltpu.make_async_copy(ref, ref, sem).wait()

    fine = order // PARTS
    rows_of = order // CHUNKS
    mesons = (m_own, m_near, m_far)

    def part_of(ref, j, i):
        return ref.at[:, pl.ds(i * fine, fine), pl.ds(pl.multiple_of(j * width, width), width)]

    direct = (odd == 1) & (c == 1)
    relays = (odd == 1) | (c == 0)
    gathers = (odd == 0) & (c == 1)
    not_direct = jnp.logical_not(direct)

    def spread(src, whole, j, i, when_near, when_far):
        send(src, part_of(m_near, j, i), near_sem(j, i), (shifted(-step_near), me), when_near, ("near", j is me), whole, EVERY)
        send(src, part_of(m_far, j, i), far_sem(j), (shifted(-step_far), me), when_far, ("direct", j is me), whole, direct)

    def own_sem(i):
        return m_sem.at[i]

    def block_sem(which, j):
        return m_sem.at[PARTS + 2 * PARTS + which * n_col + j]

    def near_sem(j, i):
        return m_sem.at[PARTS + (0 if j is me else PARTS) + i]

    def far_sem(j):
        return block_sem(2, j)

    def own(i):
        return meson.at[y, :, pl.ds(i * fine, fine), :]

    def local(src, dst, sem):
        pltpu.make_async_copy(src, dst, sem).start()

    for i in range(PARTS):
        src = meson.at[1 - y, :, pl.ds(i * fine, fine), :]
        send(src, part_of(m_own, me, i), own_sem(i), (tm, across), None, "own", meson.at[1 - y])
    for i in range(PARTS):
        spread(own(i), meson.at[y], me, i, jnp.logical_not(above(-1)), direct & jnp.logical_not(above(-3)))
    send(far.at[1 - y], columns(p_far, me), p_sem.at[1, me], (tm, across))
    send(near.at[1 - y], columns(p_near, me), p_sem.at[0, me], (tm, across))
    for src, ref, sem in ((meson, m_own, block_sem(0, me)), (far, p_far, p_sem.at[1, me]), (near, p_near, p_sem.at[0, me])):
        send(src.at[y], columns(ref, me), sem, (tm, partner))
        local(src.at[y], columns(ref, me), sem)

    rows = lax.broadcasted_iota(jnp.int32, (order, width), 0)

    def adjoint(ref, out, j):
        lanes = lax.broadcasted_iota(jnp.int32, (order, width), 1) + j * width
        sign = jnp.where((rows < half) == (lanes < half), 1.0, -1.0).astype(F32)
        first = pl.multiple_of(j * width, width)
        for part in range(2):
            block = ref[part, :, pl.ds(first, width)].astype(F32) * (sign if part == 0 else -sign)
            out[part, pl.ds(first, width), :] = jnp.transpose(block).astype(BF16)

    def mine(ref):
        picked = []
        for part in range(2):
            for k in range(2):
                picked.append(ref[part, :, pl.ds(pl.multiple_of((2 * k + c) * width, width), width)])
        return jnp.concatenate(picked, axis=1)

    def product(left, at, right):
        first = jnp.dot(left[0, at, :], right, preferred_element_type=F32)
        second = jnp.dot(left[1, at, :], right, preferred_element_type=F32)
        return first[:, :tile] - second[:, tile:], first[:, tile:] + second[:, :tile]

    def fill_inner(left, right):
        for i in range(CHUNKS):
            at = slice(i * rows_of, (i + 1) * rows_of)
            real, imag = product(left, at, right)
            inner[at, :tile] = real.astype(BF16)
            inner[at, tile:] = imag.astype(BF16)

    def piece(ref, k, i):
        return ref.at[k, :, pl.ds(i * rows_of, rows_of), :]

    def whole_meson(which):
        for j in (partner, beyond):
            wait(columns(mesons[which], j), block_sem(which, j))

    def store(out, parts, at):
        for k in range(2):
            for part in range(2):
                out[k, part, at, :] = parts[part][:, k * width:(k + 1) * width].astype(BF16)

    def run(step):
        name, *rest = step.split(".")
        if name == "drain":
            drain(True)
        elif name == "up":
            @pl.when(later > 0)
            def _():
                pl.semaphore_wait(ready, later)

            for i in range(PARTS):
                spread(own(i), meson.at[y], me, i, above(-1), direct & above(-3))
        elif name == "m0":
            i = int(rest[0])
            wait(part_of(m_own, across, i), own_sem(i))
            spread(part_of(m_own, across, i), columns(m_own, across), across, i, None, direct)
        elif name == "m0p":
            send(columns(m_own, across), columns(m_own, across), block_sem(0, across), (tm, partner))
        elif name in ("m1", "m3"):
            which = 1 if name == "m1" else 2
            ref, j = mesons[which], me if rest[0].startswith("me") else across
            if rest[0].endswith("p"):
                if which == 2:
                    wait(columns(ref, j), far_sem(j))
                send(columns(ref, j), columns(ref, j), block_sem(which, j), (tm, partner))
                return
            i = int(rest[1])
            wait(part_of(ref, j, i), near_sem(j, i))
            send(part_of(ref, j, i), part_of(m_far, j, i), far_sem(j), (shifted(-between), me), relays, ("relay", j is me), columns(ref, j))
        elif name in ("adjf1", "adjn1"):
            s, ref, out = (1, p_far, a_far) if name == "adjf1" else (0, p_near, a_near)
            for j in (me, partner):
                wait(columns(ref, j), p_sem.at[s, j])
                adjoint(ref, out, j)
        elif name in ("pf", "pn"):
            s, ref, out = (1, p_far, a_far) if name == "pf" else (0, p_near, a_near)
            wait(columns(ref, across), p_sem.at[s, across])
            send(columns(ref, across), columns(ref, across), p_sem.at[s, across], (tm, partner))
            adjoint(ref, out, across)
        elif name in ("Bf", "Bn"):
            s, ref, adj = (1, p_far, a_far) if name == "Bf" else (0, p_near, a_near)
            if name == first_backward:
                wait(columns(m_own, me), block_sem(0, me))
                whole_meson(0)
            wait(columns(ref, beyond), p_sem.at[s, beyond])
            adjoint(ref, adj, beyond)
            fill_inner(m_own, mine(adj))
            for i in range(CHUNKS):
                at = slice(i * rows_of, (i + 1) * rows_of)
                out = b_out if s else n_out
                store(out, product(ref, at, inner[...]), at)
                for k in range(2):
                    if s:
                        send(piece(out, k, i), piece(b_in, k, i), b_sem.at[k, i], (shifted(between), me), not_direct, "far", out)
                        send(piece(out, k, i), piece(bx_far, k, i), bx_sem.at[1, k, i], (shifted(step_near), me), direct, "cross far", out)
                    else:
                        send(piece(out, k, i), piece(bx_near, k, i), bx_sem.at[0, k, i], (shifted(-step_near), me), direct, "cross near", out)
        elif name == "Fn":
            whole_meson(1)
            fill_inner(m_near, mine(p_near))
            for i in range(CHUNKS):
                at = slice(i * rows_of, (i + 1) * rows_of)
                parts = product(a_near, at, inner[...])
                for part in range(2):
                    f_sum[part, at, :] = parts[part]
        elif name == "Ff":
            whole_meson(2)
            fill_inner(m_far, mine(p_far))
            for i in range(CHUNKS):
                at = slice(i * rows_of, (i + 1) * rows_of)
                parts = product(a_far, at, inner[...])
                store(f_out, (parts[0] + f_sum[0, at, :], parts[1] + f_sum[1, at, :]), at)
            send(f_out.at[1 - y], f_home.at[y], f_sem.at[0], (tm, across))
            local(f_out.at[y], f_home.at[y], f_sem.at[0])
        elif name in ("h1", "h2", "e1", "l1"):
            k, i = int(rest[0]), int(rest[1])
            at = pl.ds(i * rows_of, rows_of)
            if name != "h2":
                when, out, by = not_direct, s_out, step_near
                if name != "h1":
                    when = when & (place >= 4 if name == "e1" else place < 4)

                @pl.when(when)
                def _():
                    wait(piece(b_in, k, i), b_sem.at[k, i])
                    s_out[k, :, at, :] = (n_out[k, :, at, :].astype(F32) + b_in[k, :, at, :].astype(F32)).astype(BF16)
            else:
                when, out, by = gathers, bx_out, between

                @pl.when(when)
                def _():
                    wait(piece(bx_near, k, i), bx_sem.at[0, k, i])
                    wait(piece(bx_far, k, i), bx_sem.at[1, k, i])
                    bx_out[k, :, at, :] = (bx_near[k, :, at, :].astype(F32) + bx_far[k, :, at, :].astype(F32)).astype(BF16)

            send(piece(out, k, i), piece(b_home, y, i), bh_sem.at[0], (shifted(by), 2 * k + c), when, "h2" if name == "h2" else "h1", out, gathers if name == "h2" else not_direct)

    first_backward = min(("Bf", "Bn"), key=ORDER.index)
    for step in ORDER:
        run(step)

    wait(f_home, f_sem.at[0])
    wait(b_home, bh_sem.at[0])
    drain(False)


def shards(n_tm, n_col, near_prop, far_prop, meson):
    slices, parts, order, width = meson.shape
    whole = pltpu.VMEM((parts, order, order), BF16)
    pair = pltpu.VMEM((2, parts, order, width), BF16)
    home = jax.ShapeDtypeStruct((slices, parts, order, width), BF16)
    dma = pltpu.SemaphoreType.DMA
    forward, backward = pl.pallas_call(
        functools.partial(kernel, n_tm, n_col),
        out_shape=(home, home),
        in_specs=[pl.BlockSpec(memory_space=pl.ANY)] * 3,
        out_specs=[pl.BlockSpec(memory_space=pl.ANY)] * 2,
        scratch_shapes=[
            whole, whole, whole, whole, whole, whole, whole,
            pltpu.VMEM((order, 4 * width), BF16),
            pair, pair, pair, pair, pair, pair, pair,
            pltpu.VMEM((parts, order, 2 * width), F32), pair,
            dma((3 * PARTS + 3 * n_col,)), dma((2, n_col)), dma((2, CHUNKS)), dma((2, 2, CHUNKS)), dma((1,)), dma((1,)), dma((SENDS,)),
            pltpu.SemaphoreType.REGULAR,
        ],
        compiler_params=pltpu.CompilerParams(
            collective_id=0, has_side_effects=True, vmem_limit_bytes=105 * 512 * 1024
        ),
    )(near_prop, far_prop, meson)
    return forward.astype(F32) + backward.astype(F32)


def solution(mesh):
    spec = P("tm", None, None, "col")
    body = functools.partial(shards, mesh.shape["tm"], mesh.shape["col"])
    return jax.shard_map(body, mesh=mesh, in_specs=(spec, spec, spec), out_specs=spec, check_vma=False)
```
